32 devices in a mesh: dp: 16 (over z, x, core), tensor: 2 (over y).
Axes of the slice: x: 2, y: 2, z: 4, core: 2. Of those that a mesh axis runs over, the one named last changes fastest.
Arguments:
- tokens: bfloat16 [16384, 1024], P('dp'), may hold values from -6 to 6
- proj_weight: bfloat16 [1024, 3, 1024], P(None, None, 'tensor'), may hold values from -0.1875 to 0.1875
- query_bias: float32 [16, 64], P('tensor'), may hold values from -1.75 to 1.75
- value_bias: float32 [16, 64], P('tensor'), may hold values from -0.0625 to 0.0625
- out_weight: bfloat16 [1024, 1024], P('tensor'), may hold values from -6 to 6
- out_bias: float32 [1024], replicated, may hold values from -1.75 to 1.75
- first_gain: float32 [1024], replicated, may hold values from 0.5 to 1.5
- first_shift: float32 [1024], replicated, may hold values from -1.75 to 1.75
- up_weight: bfloat16 [1024, 4096], P(None, 'tensor'), may hold values from -0.1875 to 0.1875
- up_bias: float32 [64, 64], P('tensor'), may hold values from -3 to 3
- down_weight: bfloat16 [4096, 1024], P('tensor'), may hold values from -0.09375 to 0.09375
- down_bias: float32 [1024], replicated, may hold values from -1.75 to 1.75
- second_gain: float32 [1024], replicated, may hold values from 0.5 to 1.5
- second_shift: float32 [1024], replicated, may hold values from -1.75 to 1.75
- cotangent: bfloat16 [16384, 1024], P('dp'), may hold values from -6 to 6
Outputs:
- layer_out: bfloat16 [16384, 1024], P('dp')
- tokens_grad: float32 [16384, 1024], P('dp')
- proj_grad: float32 [1024, 3, 1024], P('dp', None, 'tensor')
- querybias_grad: float32 [16, 64], P('tensor', 'dp')
- valuebias_grad: float32 [16, 64], P('tensor', 'dp')
- outweight_grad: float32 [1024, 1024], P('tensor', 'dp')
- outbias_grad: float32 [1024], P('dp')
- firstgain_grad: float32 [1024], P('dp')
- firstshift_grad: float32 [1024], P('dp')
- upweight_grad: float32 [1024, 4096], P('dp', 'tensor')
- upbias_grad: float32 [64, 64], P('tensor', 'dp')
- downweight_grad: float32 [4096, 1024], P('tensor', 'dp')
- downbias_grad: float32 [1024], P('dp')
- secondgain_grad: float32 [1024], P('dp')
- secondshift_grad: float32 [1024], P('dp')
The draws below stay inside these ranges and needn't reach their ends.
All inputs are finite; a program needn't handle non-finite values.
Results may differ from the reference program's by a relative error of at most 0.015.
The reference program's roundings to bfloat16 on the way count: a program that leaves them out, or rounds other values in their place, can miss the bound.
Values may be sent and summed in bfloat16 or wider, within the bound.
A program may use at most 192 MiB of HBM per device.

```python
import math
import jax
import jax.numpy as jnp
from jax import lax

D = 1024
HEADS = 16
HD = 64
FF = 4096
TOK_DEV = 1024
GROUP = 4
LENGTH = 4096
TOKENS = 16384


def spiked(drawn, own_key, source, target, shards_of, factor):
    def block_of(position):
        return (jnp.arange(drawn.shape[position]) // (drawn.shape[position] // shards_of)).reshape((-1,) + (1,) * (drawn.ndim - 1 - position))

    one_side = jax.random.permutation(own_key, shards_of)[block_of(target)]
    second = (block_of(target) + shards_of // 2) % shards_of
    return jnp.where((block_of(source) == one_side) | (block_of(source) == second), factor * drawn, drawn)


def block_levels(stream_key, dims, pieces, least, high):
    level, own = 1.0, jax.random.fold_in(stream_key, 6)
    for dim, shards_of in pieces:
        steps = jnp.exp(jax.random.uniform(jax.random.fold_in(own, dim), (shards_of,), jnp.float32, least / len(pieces), high / len(pieces)))
        level = level * jnp.repeat(steps, dims[dim] // shards_of).reshape([-1 if axis == dim else 1 for axis in range(len(dims))])
    return level


def normal_values(stream_key, extent, scale, most, pieces=(), dtype=jnp.bfloat16):
    result = scale * jax.random.normal(stream_key, extent, jnp.float32)
    if pieces:
        result = result * block_levels(stream_key, extent, pieces, -0.22, 0.18)
    return jnp.clip(result, -most, most).astype(dtype)


def heavy_noise(rng, dims, scale, bound, split, heavy, kind=jnp.bfloat16):
    values = scale * jax.random.normal(rng, dims, jnp.float32)
    if split:
        values = values * block_levels(rng, dims, split, -0.22, 0.18)
    return jnp.clip(spiked(values, jax.random.fold_in(rng, 3), *heavy), -bound, bound).astype(kind)


def setup_inputs(seed: int = 0) -> dict:
    streams_of = jax.random.split(jax.random.key(seed), 16)
    tokens = heavy_noise(streams_of[0], (TOKENS, D), 1.0, 6.0, ((0, 16),), (0, 1, 16, 2.0))
    proj_weight = normal_values(streams_of[1], (D, 3, D), D ** -0.5, 0.1875, ((2, 2),))
    query_bias = normal_values(streams_of[2], (HEADS, HD), 0.3, 1.75, ((0, 2),), jnp.float32)
    value_bias = normal_values(streams_of[3], (HEADS, HD), 0.01, 0.0625, ((0, 2),), jnp.float32)
    out_weight = normal_values(streams_of[4], (D, D), (max(1, D * 4 // (GROUP * TOK_DEV))) ** -0.5, 6.0, ((0, 2),))
    out_bias = normal_values(streams_of[5], (D,), 0.3, 1.75, (), jnp.float32)
    first_gain = jnp.clip(1.0 + 0.1 * jax.random.normal(streams_of[6], (D,), jnp.float32), 0.5, 1.5)
    first_shift = normal_values(streams_of[7], (D,), 0.3, 1.75, (), jnp.float32)
    up_weight = normal_values(streams_of[8], (D, FF), D ** -0.5, 0.1875, ((1, 2),))
    up_bias = normal_values(streams_of[9], (FF // HD, HD), 0.5, 3.0, ((0, 2),), jnp.float32)
    down_weight = normal_values(streams_of[10], (FF, D), FF ** -0.5, 0.09375, ((0, 2),))
    down_bias = normal_values(streams_of[11], (D,), 0.3, 1.75, (), jnp.float32)
    second_gain = jnp.clip(1.0 + 0.1 * jax.random.normal(streams_of[12], (D,), jnp.float32), 0.5, 1.5)
    second_shift = normal_values(streams_of[13], (D,), 0.3, 1.75, (), jnp.float32)
    cotangent = heavy_noise(streams_of[14], (TOKENS, D), 1.0, 6.0, ((0, 16),), (0, 1, 16, 2.0))
    return {"tokens": tokens, "proj_weight": proj_weight, "query_bias": query_bias, "value_bias": value_bias, "out_weight": out_weight, "out_bias": out_bias, "first_gain": first_gain, "first_shift": first_shift, "up_weight": up_weight, "up_bias": up_bias, "down_weight": down_weight, "down_bias": down_bias, "second_gain": second_gain, "second_shift": second_shift, "cotangent": cotangent}


@jax.custom_vjp
def low(v):
    return lax.optimization_barrier(v.astype(jnp.bfloat16)).astype(jnp.float32)

@jax.custom_vjp
def low_back(v):
    return v

def low_keep(v):
    return (low(v), None)

def low_pass(kept, grad):
    return (grad,)

def back_keep(v):
    return (v, None)

def back_low(kept, grad):
    return (low(grad),)
low.defvjp(low_keep, low_pass)
low_back.defvjp(back_keep, back_low)
EPS = 1e-12

def matmul(left, right):
    return jnp.dot(left, right, precision=lax.Precision.HIGHEST, preferred_element_type=jnp.float32)

def layer_norm(rows, gain, shift):
    mean = lax.optimization_barrier(jnp.mean(rows, axis=-1, keepdims=True))
    centered = rows - mean
    spread = lax.optimization_barrier(jnp.mean(centered * centered, axis=-1, keepdims=True))
    return centered * lax.rsqrt(spread + EPS) * gain + shift

def heads_first(rows):
    return rows.reshape(rows.shape[0], HEADS, HD).transpose(1, 0, 2)

def one_head(parts):
    query_head, key_head, value_head = parts
    scale = 1.0 / math.sqrt(HD)
    scores = low_back(matmul(query_head, key_head.T) * scale)
    probs = low(jax.nn.softmax(scores, axis=-1))
    return matmul(probs, value_head)

def attend(queries, keys, values):
    context = lax.map(jax.checkpoint(one_head), (heads_first(queries), heads_first(keys), heads_first(values)))
    return context.transpose(1, 0, 2).reshape(queries.shape[0], D)

def sequence(params, rows):
    proj_w, query_b, value_b, out_w, out_b, gain_one, shift_one, up_w, up_b, down_w, down_b, gain_two, shift_two = params
    mixed = matmul(rows, proj_w.reshape(D, 3 * D))
    queries = low_back(low(mixed[:, :D] + query_b.reshape(D)))
    keys = low_back(low(mixed[:, D:2 * D]))
    values = low_back(low(mixed[:, 2 * D:] + value_b.reshape(D)))
    context = low_back(low(attend(queries, keys, values)))
    attention = low_back(matmul(context, out_w) + out_b)
    first = layer_norm(rows + attention, gain_one, shift_one)
    hidden = low_back(matmul(low(first), up_w) + up_b.reshape(FF))
    active = low(jax.nn.gelu(hidden, approximate=True))
    feed = low_back(matmul(active, down_w) + down_b)
    return layer_norm(first + feed, gain_two, shift_two)

def forward(params, rows_all):
    blocks = rows_all.reshape(TOKENS // LENGTH, LENGTH, D)
    outputs = lax.map(lambda rows: sequence(params, rows), blocks)
    return outputs.reshape(TOKENS, D)

def reference(tokens, proj_weight, query_bias, value_bias, out_weight, out_bias, first_gain, first_shift, up_weight, up_bias, down_weight, down_bias, second_gain, second_shift, cotangent):
    params = (proj_weight.astype(jnp.float32), query_bias.astype(jnp.float32), value_bias.astype(jnp.float32), out_weight.astype(jnp.float32), out_bias.astype(jnp.float32), first_gain.astype(jnp.float32), first_shift.astype(jnp.float32), up_weight.astype(jnp.float32), up_bias.astype(jnp.float32), down_weight.astype(jnp.float32), down_bias.astype(jnp.float32), second_gain.astype(jnp.float32), second_shift.astype(jnp.float32))
    layer, pullback = jax.vjp(forward, params, tokens.astype(jnp.float32))
    grads, tokens_grad = pullback(cotangent.astype(jnp.float32))
    return (layer.astype(jnp.bfloat16), tokens_grad, grads[0], grads[1], grads[2], grads[3], grads[4], grads[5], grads[6], grads[7], grads[8], grads[9], grads[10], grads[11], grads[12])
```

```python
import functools
import math

import jax
import jax.numpy as jnp
from jax import lax
from jax.experimental import pallas as pl
from jax.experimental.pallas import tpu as pltpu
from jax.sharding import PartitionSpec as P

EPS = 1e-12
F32 = jnp.float32
BF16 = jnp.bfloat16
LANES = 128
HALF = 64
SOURCES = 4
CHUNKS = 2
NN = (((1,), (0,)), ((), ()))
NT = (((1,), (1,)), ((), ()))
TN = (((0,), (0,)), ((), ()))


def dot(left, right, dims):
    return lax.dot_general(left, right, dims, preferred_element_type=F32)


def flip(value, axis, bit):
    pairs = [(source, source ^ (1 << bit)) for source in range(lax.axis_size(axis))]
    return lax.ppermute(value, axis, pairs)


def pair_sum(partial):
    low = partial.astype(BF16)
    return low.astype(F32) + flip(low, "tensor", 0).astype(F32)


def scatter_rows(rows, wire):
    size = lax.axis_size("dp")
    mine = lax.axis_index("dp")
    part = rows.shape[0] // size
    whole = rows
    bit = 0
    while size > 1:
        size //= 2
        split = whole.reshape(size, 2, part, -1)
        own = mine >> bit & 1
        keep = lax.dynamic_index_in_dim(split, own, 1, keepdims=False)
        send = lax.dynamic_index_in_dim(split, 1 - own, 1, keepdims=False)
        whole = keep.astype(F32) + flip(send.astype(wire), "dp", bit).astype(F32)
        bit += 1
    return whole.reshape(part, -1)


def layer_norm(rows, gain, shift):
    mean = jnp.mean(rows, axis=-1, keepdims=True)
    centered = rows - mean
    spread = jnp.mean(centered * centered, axis=-1, keepdims=True)
    return centered * lax.rsqrt(spread + EPS) * gain + shift


def gelu_tanh(values):
    return jax.nn.gelu(values, approximate=True)


def head_lanes(shape, head):
    lane = lax.broadcasted_iota(jnp.int32, shape, 1)
    return (lane < HALF) if head == 0 else (lane >= HALF)


def forward_kernel(scale, tile, *refs):
    q_ref = refs[0]
    k_refs = refs[1 : 1 + SOURCES]
    v_refs = refs[1 + SOURCES : 1 + 2 * SOURCES]
    o_ref, lse_ref, s_ref, vt_ref = refs[1 + 2 * SOURCES :]
    span = k_refs[0].shape[0]

    @pl.when(pl.program_id(0) == 0)
    def _():
        for source in range(SOURCES):
            vt_ref[:LANES, source * span : (source + 1) * span] = jnp.transpose(
                v_refs[source][...]
            )
        vt_ref[LANES:, :] = jnp.ones((vt_ref.shape[0] - LANES, vt_ref.shape[1]), BF16)

    q = q_ref[...] * scale
    outs = []
    for head in range(2):
        own = head_lanes(q.shape, head)
        qt = jnp.transpose(jnp.where(own, q, jnp.zeros_like(q)))
        peak = None
        for source in range(SOURCES):
            for start in range(0, span, tile):
                scores = dot(k_refs[source][start : start + tile, :], qt, NN)
                base = source * span + start
                s_ref[head, base : base + tile, :] = scores
                top = jnp.max(scores, axis=0, keepdims=True)
                peak = top if peak is None else jnp.maximum(peak, top)
        total = None
        for start in range(0, SOURCES * span, tile):
            weights = jnp.exp(s_ref[head, start : start + tile, :] - peak).astype(BF16)
            part = dot(vt_ref[:, start : start + tile], weights, NN)
            total = part if total is None else total + part
        mass = total[LANES : LANES + 1, :]
        outs.append(total[head * HALF : (head + 1) * HALF, :] / mass)
        lse_ref[head, :] = (peak + jnp.log(mass))[0]
    o_ref[...] = jnp.transpose(jnp.concatenate(outs, 0))


def attend(queries, group, blocks, scale):
    rows = queries.shape[0]
    span = blocks[0].shape[0]
    tq = rows // 2
    keys = SOURCES * span
    return pl.pallas_call(
        functools.partial(forward_kernel, scale, span // 2),
        grid=(rows // tq,),
        in_specs=[pl.BlockSpec((tq, LANES), lambda i: (i, group))]
        + [pl.BlockSpec((span, LANES), lambda i: (0, 0))] * SOURCES
        + [pl.BlockSpec((span, LANES), lambda i: (0, 1))] * SOURCES,
        out_specs=[
            pl.BlockSpec((tq, LANES), lambda i: (i, 0)),
            pl.BlockSpec((2, tq), lambda i: (0, i)),
        ],
        out_shape=[
            jax.ShapeDtypeStruct((rows, LANES), F32),
            jax.ShapeDtypeStruct((2, rows), F32),
        ],
        scratch_shapes=[
            pltpu.VMEM((2, keys, tq), F32),
            pltpu.VMEM((LANES + 16, keys), BF16),
        ],
        compiler_params=pltpu.CompilerParams(vmem_limit_bytes=40 << 20),
        cost_estimate=pl.CostEstimate(
            flops=16 * rows * keys * LANES,
            bytes_accessed=4 * (keys + rows) * LANES + 4 * rows * LANES,
            transcendentals=2 * rows * keys,
        ),
        name="attend",
    )(queries, *blocks, *blocks)


def thirds(value):
    high = value.astype(BF16).astype(F32)
    rest = value - high
    middle = rest.astype(BF16).astype(F32)
    return high, middle, rest - middle


def backward_kernel(scale, tile, *refs):
    q_ref, g_ref, o_ref, lse_ref = refs[:4]
    k_refs = refs[4 : 4 + SOURCES]
    v_refs = refs[4 + SOURCES : 4 + 2 * SOURCES]
    dq_ref = refs[4 + 2 * SOURCES]
    d_refs = refs[5 + 2 * SOURCES : 5 + 3 * SOURCES]
    qt_ref, gt_ref, dqt_ref, k_ref, v_ref, d_ref = refs[5 + 3 * SOURCES :]
    step = pl.program_id(0)
    rows = q_ref.shape[0]
    span = k_ref.shape[0]

    @pl.when(step == 0)
    def _():
        q = q_ref[...] * scale
        g = g_ref[...]
        products = jnp.transpose(g.astype(F32) * o_ref[...])
        row = lax.broadcasted_iota(jnp.int32, (LANES, rows), 0)
        for head in range(2):
            own = head_lanes(q.shape, head)
            qt_ref[head, :LANES, :] = jnp.transpose(jnp.where(own, q, jnp.zeros_like(q)))
            gt_ref[head, :LANES, :] = jnp.transpose(jnp.where(own, g, jnp.zeros_like(g)))
            centre = jnp.sum(
                products[head * HALF : (head + 1) * HALF], axis=0, keepdims=True
            )
            for ref, value in (
                (qt_ref, -lse_ref[head : head + 1, :]),
                (gt_ref, -centre),
            ):
                high, middle, low = thirds(value)
                ref[head, LANES:, :] = jnp.where(
                    row == 0,
                    high,
                    jnp.where(row == 1, middle, jnp.where(row == 2, low, 0.0)),
                ).astype(BF16)
        dqt_ref[...] = jnp.zeros_like(dqt_ref)

    for source in range(SOURCES):

        @pl.when(step == source)
        def _():
            k_ref[...] = k_refs[source][...]
            v_ref[...] = v_refs[source][...]

    for start in range(0, span, tile):
        k = k_ref[start : start + tile, :]
        v = v_ref[start : start + tile, :]
        one = jnp.ones_like(k)
        k_wide = jnp.concatenate([k, one], 1)
        v_wide = jnp.concatenate([v, one], 1)
        kt = jnp.transpose(k)
        parts = []
        for head in range(2):
            probs = jnp.exp(dot(k_wide, qt_ref[head], NN))
            centred = dot(v_wide, gt_ref[head], NN)
            score_grad = (probs * centred).astype(BF16)
            parts.append(
                (
                    dot(score_grad, q_ref[...], NN),
                    dot(probs.astype(BF16), g_ref[...], NN),
                )
            )
            dqt_ref[head * HALF : (head + 1) * HALF, :] += dot(
                kt[head * HALF : (head + 1) * HALF, :], score_grad, NN
            )
        first = head_lanes(k.shape, 0)
        d_ref[start : start + tile, :LANES] = (
            jnp.where(first, parts[0][0], parts[1][0]) * scale
        ).astype(BF16)
        d_ref[start : start + tile, LANES:] = jnp.where(
            first, parts[0][1], parts[1][1]
        ).astype(BF16)

    for source in range(SOURCES):

        @pl.when(step == source)
        def _():
            d_refs[source][...] = d_ref[...]

    @pl.when(step == SOURCES - 1)
    def _():
        dq_ref[...] = (jnp.transpose(dqt_ref[...]) * scale).astype(BF16)


def attend_back(queries, grads, group, context, lse, blocks, scale):
    rows = queries.shape[0]
    span = blocks[0].shape[0]
    keys = SOURCES * span
    whole = lambda i: (0, 0)
    return pl.pallas_call(
        functools.partial(backward_kernel, scale, span // 2),
        grid=(SOURCES,),
        in_specs=[
            pl.BlockSpec((rows, LANES), lambda i: (0, group)),
            pl.BlockSpec((rows, LANES), lambda i: (0, group)),
            pl.BlockSpec((rows, LANES), whole),
            pl.BlockSpec((2, rows), whole),
        ]
        + [pl.BlockSpec((span, LANES), whole)] * SOURCES
        + [pl.BlockSpec((span, LANES), lambda i: (0, 1))] * SOURCES,
        out_specs=[pl.BlockSpec((rows, LANES), whole)]
        + [pl.BlockSpec((span, 2 * LANES), whole)] * SOURCES,
        out_shape=[jax.ShapeDtypeStruct((rows, LANES), BF16)]
        + [jax.ShapeDtypeStruct((span, 2 * LANES), BF16)] * SOURCES,
        scratch_shapes=[
            pltpu.VMEM((2, 2 * LANES, rows), BF16),
            pltpu.VMEM((2, 2 * LANES, rows), BF16),
            pltpu.VMEM((LANES, rows), F32),
            pltpu.VMEM((span, LANES), BF16),
            pltpu.VMEM((span, LANES), BF16),
            pltpu.VMEM((span, 2 * LANES), BF16),
        ],
        compiler_params=pltpu.CompilerParams(vmem_limit_bytes=40 << 20),
        cost_estimate=pl.CostEstimate(
            flops=28 * rows * keys * LANES,
            bytes_accessed=8 * keys * LANES + 12 * rows * LANES,
            transcendentals=2 * rows * keys,
        ),
        name="attend_back",
    )(queries, grads, context, lse, *blocks, *blocks)


def body(
    tokens,
    proj_weight,
    query_bias,
    value_bias,
    out_weight,
    out_bias,
    first_gain,
    first_shift,
    up_weight,
    up_bias,
    down_weight,
    down_bias,
    second_gain,
    second_shift,
    cotangent,
):
    rows, width = tokens.shape
    heads, head_size = query_bias.shape
    local = heads * head_size
    groups = local // LANES
    scale = 1.0 / math.sqrt(head_size)
    query_weight = proj_weight[:, 0, :]
    key_weight = proj_weight[:, 1, :]
    value_weight = proj_weight[:, 2, :]
    value_shift = value_bias.reshape(local)

    own_blocks, blocks = [], []
    for group in range(groups):
        cols = slice(group * LANES, (group + 1) * LANES)
        weight = jnp.concatenate([key_weight[:, cols], value_weight[:, cols]], axis=1)
        shift = jnp.concatenate([jnp.zeros((LANES,), F32), value_shift[cols]])
        own_blocks.append((dot(tokens, weight, NN) + shift).astype(BF16))
    for own in own_blocks:
        across = flip(own, "dp", 1)
        blocks.append((own, flip(own, "dp", 0), across, flip(across, "dp", 0)))
    queries = (dot(tokens, query_weight, NN) + query_bias.reshape(local)).astype(BF16)

    outs = [attend(queries, group, blocks[group], scale) for group in range(groups)]
    context = jnp.concatenate([out.astype(BF16) for out, _ in outs], axis=1)

    step = rows // CHUNKS
    cuts = [slice(i * step, (i + 1) * step) for i in range(CHUNKS)]
    attentions = [pair_sum(dot(context[cut], out_weight, NN)) + out_bias for cut in cuts]
    firsts = [
        jax.vjp(layer_norm, tokens[cut].astype(F32) + attention, first_gain, first_shift)
        for cut, attention in zip(cuts, attentions)
    ]
    lows = [first.astype(BF16) for first, _ in firsts]
    hiddens = [dot(low, up_weight, NN) + up_bias.reshape(-1) for low in lows]
    actives = [jax.vjp(gelu_tanh, hidden) for hidden in hiddens]
    active_lows = [active.astype(BF16) for active, _ in actives]
    feeds = [pair_sum(dot(active, down_weight, NN)) + down_bias for active in active_lows]
    seconds = [
        jax.vjp(layer_norm, first + feed, second_gain, second_shift)
        for (first, _), feed in zip(firsts, feeds)
    ]
    layer_output = jnp.concatenate([second.astype(BF16) for second, _ in seconds], axis=0)
    second_grads = [
        back(cotangent[cut].astype(F32)) for cut, (_, back) in zip(cuts, seconds)
    ]
    feed_grads = [grads[0].astype(BF16) for grads in second_grads]
    hidden_lows = [
        back(dot(feed_grad, down_weight, NT))[0].astype(BF16)
        for feed_grad, (_, back) in zip(feed_grads, actives)
    ]
    first_grads = [
        grads[0] + pair_sum(dot(low, up_weight, NT))
        for grads, low in zip(second_grads, hidden_lows)
    ]
    feed_grad = jnp.concatenate(feed_grads, axis=0)
    hidden_low = jnp.concatenate(hidden_lows, axis=0)
    active_low = jnp.concatenate(active_lows, axis=0)
    first_low = jnp.concatenate(lows, axis=0)
    downweight_grad = scatter_rows(dot(feed_grad, active_low, TN).astype(BF16), BF16)
    upweight_grad = scatter_rows(dot(first_low, hidden_low, TN).astype(BF16), BF16)
    downbias_grad = jnp.sum(feed_grad.astype(F32), axis=0)
    upbias_grad = jnp.sum(hidden_low.astype(F32), axis=0)
    secondgain_grad = sum(grads[1] for grads in second_grads)
    secondshift_grad = sum(grads[2] for grads in second_grads)

    back_grads = [back(grad) for grad, (_, back) in zip(first_grads, firsts)]
    attention_back = jnp.concatenate([grads[0] for grads in back_grads], axis=0)
    firstgain_grad = sum(grads[1] for grads in back_grads)
    firstshift_grad = sum(grads[2] for grads in back_grads)
    attention_grad = attention_back.astype(BF16)
    outbias_grad = jnp.sum(attention_grad.astype(F32), axis=0)
    outweight_grad = scatter_rows(dot(attention_grad, context, TN).astype(BF16), BF16)
    context_grad = dot(attention_grad, out_weight, NT).astype(BF16)

    query_grads, key_grads, value_grads = [], [], []
    for group in range(groups):
        out, lse = outs[group]
        query_part, own, beside, across, diagonal = attend_back(
            queries, context_grad, group, out, lse, blocks[group], scale
        )
        here = own.astype(F32) + flip(beside, "dp", 0).astype(F32)
        there = across.astype(F32) + flip(diagonal, "dp", 0).astype(F32)
        total = (here + flip(there.astype(BF16), "dp", 1).astype(F32)).astype(BF16)
        query_grads.append(query_part)
        key_grads.append(total[:, :LANES])
        value_grads.append(total[:, LANES:])
    joined_grads = jnp.concatenate(query_grads + key_grads + value_grads, axis=1)
    flat_proj = jnp.concatenate([query_weight, key_weight, value_weight], axis=1)
    proj_grad = scatter_rows(dot(tokens, joined_grads, TN).astype(BF16), BF16)
    bias_grads = jnp.sum(joined_grads.astype(F32), axis=0)
    tokens_grad = attention_back + pair_sum(dot(joined_grads, flat_proj, NT))

    size = lax.axis_size("dp")

    def by_dp(vector, leading):
        return (
            vector.reshape(leading, size, -1).transpose(1, 0, 2).reshape(size, -1)
        )

    units = up_bias.shape[0]
    small = [
        (by_dp(bias_grads[:local], heads), heads),
        (by_dp(bias_grads[2 * local :], heads), heads),
        (by_dp(outbias_grad, 1), 0),
        (by_dp(firstgain_grad, 1), 0),
        (by_dp(firstshift_grad, 1), 0),
        (by_dp(upbias_grad, units), units),
        (by_dp(downbias_grad, 1), 0),
        (by_dp(secondgain_grad, 1), 0),
        (by_dp(secondshift_grad, 1), 0),
    ]
    packed = scatter_rows(jnp.concatenate([part for part, _ in small], axis=1), F32)[0]
    vectors, at = [], 0
    for part, leading in small:
        piece = packed[at : at + part.shape[1]]
        at += part.shape[1]
        vectors.append(piece.reshape(leading, -1) if leading else piece)
    return (
        layer_output,
        tokens_grad,
        proj_grad.reshape(width // size, 3, local),
        vectors[0],
        vectors[1],
        outweight_grad.T,
        vectors[2],
        vectors[3],
        vectors[4],
        upweight_grad,
        vectors[5],
        downweight_grad.T,
        vectors[6],
        vectors[7],
        vectors[8],
    )


def solution(mesh):
    return jax.shard_map(
        body,
        mesh=mesh,
        in_specs=(
            P("dp", None),
            P(None, None, "tensor"),
            P("tensor", None),
            P("tensor", None),
            P("tensor", None),
            P(),
            P(),
            P(),
            P(None, "tensor"),
            P("tensor", None),
            P("tensor", None),
            P(),
            P(),
            P(),
            P("dp", None),
        ),
        out_specs=(
            P("dp", None),
            P("dp", None),
            P("dp", None, "tensor"),
            P("tensor", "dp"),
            P("tensor", "dp"),
            P("tensor", "dp"),
            P("dp"),
            P("dp"),
            P("dp"),
            P("dp", "tensor"),
            P("tensor", "dp"),
            P("tensor", "dp"),
            P("dp"),
            P("dp"),
            P("dp"),
        ),
        check_vma=False,
    )
```

```python
import functools
import math

import jax
import jax.numpy as jnp
from jax import lax
from jax.experimental import pallas as pl
from jax.experimental.pallas import tpu as pltpu
from jax.sharding import PartitionSpec as P

EPS = 1e-12
F32 = jnp.float32
BF16 = jnp.bfloat16
LANES = 128
HALF = 64
SOURCES = 4
CHUNKS = 2
NN = (((1,), (0,)), ((), ()))
NT = (((1,), (1,)), ((), ()))
TN = (((0,), (0,)), ((), ()))


def dot(left, right, dims):
    return lax.dot_general(left, right, dims, preferred_element_type=F32)


def flip(value, axis, bit):
    pairs = [(source, source ^ (1 << bit)) for source in range(lax.axis_size(axis))]
    return lax.ppermute(value, axis, pairs)


def pair_sum(partial):
    low = partial.astype(BF16)
    return low.astype(F32) + flip(low, "tensor", 0).astype(F32)


def after(value, *earlier):
    return lax.optimization_barrier((value, earlier))[0]


class Scatter:
    def __init__(self, rows, wire):
        self.size = lax.axis_size("dp")
        self.part = rows.shape[0] // self.size
        self.whole = rows
        self.wire = wire
        self.bit = 0
        self.flight = None
        self.launch()

    def launch(self):
        if self.size == 1:
            return
        self.size //= 2
        split = self.whole.reshape(self.size, 2, self.part, -1)
        own = lax.axis_index("dp") >> self.bit & 1
        self.keep = lax.dynamic_index_in_dim(split, own, 1, keepdims=False)
        send = lax.dynamic_index_in_dim(split, 1 - own, 1, keepdims=False)
        self.flight = flip(send.astype(self.wire), "dp", self.bit)
        self.bit += 1

    def land(self, *earlier):
        if self.flight is None:
            return self.whole
        flight = after(self.flight, *earlier) if earlier else self.flight
        self.whole = self.keep.astype(F32) + flight.astype(F32)
        self.flight = None
        self.launch()
        return self.whole

    def result(self):
        while self.flight is not None:
            self.land()
        return self.whole.reshape(self.part, -1)


def layer_norm(rows, gain, shift):
    mean = jnp.mean(rows, axis=-1, keepdims=True)
    centered = rows - mean
    spread = jnp.mean(centered * centered, axis=-1, keepdims=True)
    return centered * lax.rsqrt(spread + EPS) * gain + shift


def gelu_tanh(values):
    return jax.nn.gelu(values, approximate=True)


def head_lanes(shape, head):
    lane = lax.broadcasted_iota(jnp.int32, shape, 1)
    return (lane < HALF) if head == 0 else (lane >= HALF)


def forward_kernel(scale, tile, *refs):
    q_ref = refs[0]
    k_refs = refs[1 : 1 + SOURCES]
    v_refs = refs[1 + SOURCES : 1 + 2 * SOURCES]
    o_ref, lse_ref, s_ref, vt_ref = refs[1 + 2 * SOURCES :]
    span = k_refs[0].shape[0]

    @pl.when(pl.program_id(0) == 0)
    def _():
        for source in range(SOURCES):
            vt_ref[:LANES, source * span : (source + 1) * span] = jnp.transpose(
                v_refs[source][...]
            )
        vt_ref[LANES:, :] = jnp.ones((vt_ref.shape[0] - LANES, vt_ref.shape[1]), BF16)

    q = q_ref[...] * scale
    outs = []
    for head in range(2):
        own = head_lanes(q.shape, head)
        qt = jnp.transpose(jnp.where(own, q, jnp.zeros_like(q)))
        peak = None
        for source in range(SOURCES):
            for start in range(0, span, tile):
                scores = dot(k_refs[source][start : start + tile, :], qt, NN)
                base = source * span + start
                s_ref[head, base : base + tile, :] = scores
                top = jnp.max(scores, axis=0, keepdims=True)
                peak = top if peak is None else jnp.maximum(peak, top)
        total = None
        for start in range(0, SOURCES * span, tile):
            weights = jnp.exp(s_ref[head, start : start + tile, :] - peak).astype(BF16)
            part = dot(vt_ref[:, start : start + tile], weights, NN)
            total = part if total is None else total + part
        mass = total[LANES : LANES + 1, :]
        outs.append(total[head * HALF : (head + 1) * HALF, :] / mass)
        lse_ref[head, :] = (peak + jnp.log(mass))[0]
    o_ref[...] = jnp.transpose(jnp.concatenate(outs, 0))


def attend(queries, group, blocks, scale):
    rows = queries.shape[0]
    span = blocks[0].shape[0]
    tq = rows // 2
    keys = SOURCES * span
    return pl.pallas_call(
        functools.partial(forward_kernel, scale, span // 2),
        grid=(rows // tq,),
        in_specs=[pl.BlockSpec((tq, LANES), lambda i: (i, group))]
        + [pl.BlockSpec((span, LANES), lambda i: (0, 0))] * SOURCES
        + [pl.BlockSpec((span, LANES), lambda i: (0, 1))] * SOURCES,
        out_specs=[
            pl.BlockSpec((tq, LANES), lambda i: (i, 0)),
            pl.BlockSpec((2, tq), lambda i: (0, i)),
        ],
        out_shape=[
            jax.ShapeDtypeStruct((rows, LANES), F32),
            jax.ShapeDtypeStruct((2, rows), F32),
        ],
        scratch_shapes=[
            pltpu.VMEM((2, keys, tq), F32),
            pltpu.VMEM((LANES + 16, keys), BF16),
        ],
        compiler_params=pltpu.CompilerParams(vmem_limit_bytes=40 << 20),
        cost_estimate=pl.CostEstimate(
            flops=16 * rows * keys * LANES,
            bytes_accessed=4 * (keys + rows) * LANES + 4 * rows * LANES,
            transcendentals=2 * rows * keys,
        ),
        name="attend",
    )(queries, *blocks, *blocks)


def thirds(value):
    high = value.astype(BF16).astype(F32)
    rest = value - high
    middle = rest.astype(BF16).astype(F32)
    return high, middle, rest - middle


def backward_kernel(scale, tile, *refs):
    q_ref, g_ref, o_ref, lse_ref = refs[:4]
    k_refs = refs[4 : 4 + SOURCES]
    v_refs = refs[4 + SOURCES : 4 + 2 * SOURCES]
    dq_ref = refs[4 + 2 * SOURCES]
    d_refs = refs[5 + 2 * SOURCES : 5 + 3 * SOURCES]
    qt_ref, gt_ref, dqt_ref, k_ref, v_ref, d_ref = refs[5 + 3 * SOURCES :]
    step = pl.program_id(0)
    rows = q_ref.shape[0]
    span = k_ref.shape[0]

    @pl.when(step == 0)
    def _():
        q = q_ref[...] * scale
        g = g_ref[...]
        products = jnp.transpose(g.astype(F32) * o_ref[...])
        row = lax.broadcasted_iota(jnp.int32, (LANES, rows), 0)
        for head in range(2):
            own = head_lanes(q.shape, head)
            qt_ref[head, :LANES, :] = jnp.transpose(jnp.where(own, q, jnp.zeros_like(q)))
            gt_ref[head, :LANES, :] = jnp.transpose(jnp.where(own, g, jnp.zeros_like(g)))
            centre = jnp.sum(
                products[head * HALF : (head + 1) * HALF], axis=0, keepdims=True
            )
            for ref, value in (
                (qt_ref, -lse_ref[head : head + 1, :]),
                (gt_ref, -centre),
            ):
                high, middle, low = thirds(value)
                ref[head, LANES:, :] = jnp.where(
                    row == 0,
                    high,
                    jnp.where(row == 1, middle, jnp.where(row == 2, low, 0.0)),
                ).astype(BF16)
        dqt_ref[...] = jnp.zeros_like(dqt_ref)

    for source in range(SOURCES):

        @pl.when(step == source)
        def _():
            k_ref[...] = k_refs[source][...]
            v_ref[...] = v_refs[source][...]

    for start in range(0, span, tile):
        k = k_ref[start : start + tile, :]
        v = v_ref[start : start + tile, :]
        one = jnp.ones_like(k)
        k_wide = jnp.concatenate([k, one], 1)
        v_wide = jnp.concatenate([v, one], 1)
        kt = jnp.transpose(k)
        parts = []
        for head in range(2):
            probs = jnp.exp(dot(k_wide, qt_ref[head], NN))
            centred = dot(v_wide, gt_ref[head], NN)
            score_grad = (probs * centred).astype(BF16)
            parts.append(
                (
                    dot(score_grad, q_ref[...], NN),
                    dot(probs.astype(BF16), g_ref[...], NN),
                )
            )
            dqt_ref[head * HALF : (head + 1) * HALF, :] += dot(
                kt[head * HALF : (head + 1) * HALF, :], score_grad, NN
            )
        first = head_lanes(k.shape, 0)
        d_ref[start : start + tile, :LANES] = (
            jnp.where(first, parts[0][0], parts[1][0]) * scale
        ).astype(BF16)
        d_ref[start : start + tile, LANES:] = jnp.where(
            first, parts[0][1], parts[1][1]
        ).astype(BF16)

    for source in range(SOURCES):

        @pl.when(step == source)
        def _():
            d_refs[source][...] = d_ref[...]

    @pl.when(step == SOURCES - 1)
    def _():
        dq_ref[...] = (jnp.transpose(dqt_ref[...]) * scale).astype(BF16)


def attend_back(queries, grads, group, context, lse, blocks, scale):
    rows = queries.shape[0]
    span = blocks[0].shape[0]
    keys = SOURCES * span
    whole = lambda i: (0, 0)
    return pl.pallas_call(
        functools.partial(backward_kernel, scale, span // 2),
        grid=(SOURCES,),
        in_specs=[
            pl.BlockSpec((rows, LANES), lambda i: (0, group)),
            pl.BlockSpec((rows, LANES), lambda i: (0, group)),
            pl.BlockSpec((rows, LANES), whole),
            pl.BlockSpec((2, rows), whole),
        ]
        + [pl.BlockSpec((span, LANES), whole)] * SOURCES
        + [pl.BlockSpec((span, LANES), lambda i: (0, 1))] * SOURCES,
        out_specs=[pl.BlockSpec((rows, LANES), whole)]
        + [pl.BlockSpec((span, 2 * LANES), whole)] * SOURCES,
        out_shape=[jax.ShapeDtypeStruct((rows, LANES), BF16)]
        + [jax.ShapeDtypeStruct((span, 2 * LANES), BF16)] * SOURCES,
        scratch_shapes=[
            pltpu.VMEM((2, 2 * LANES, rows), BF16),
            pltpu.VMEM((2, 2 * LANES, rows), BF16),
            pltpu.VMEM((LANES, rows), F32),
            pltpu.VMEM((span, LANES), BF16),
            pltpu.VMEM((span, LANES), BF16),
            pltpu.VMEM((span, 2 * LANES), BF16),
        ],
        compiler_params=pltpu.CompilerParams(vmem_limit_bytes=40 << 20),
        cost_estimate=pl.CostEstimate(
            flops=28 * rows * keys * LANES,
            bytes_accessed=8 * keys * LANES + 12 * rows * LANES,
            transcendentals=2 * rows * keys,
        ),
        name="attend_back",
    )(queries, grads, context, lse, *blocks, *blocks)


def body(
    tokens,
    proj_weight,
    query_bias,
    value_bias,
    out_weight,
    out_bias,
    first_gain,
    first_shift,
    up_weight,
    up_bias,
    down_weight,
    down_bias,
    second_gain,
    second_shift,
    cotangent,
):
    rows, width = tokens.shape
    heads, head_size = query_bias.shape
    local = heads * head_size
    groups = local // LANES
    scale = 1.0 / math.sqrt(head_size)
    query_weight = proj_weight[:, 0, :]
    key_weight = proj_weight[:, 1, :]
    value_weight = proj_weight[:, 2, :]
    value_shift = value_bias.reshape(local)

    side = lax.axis_index("tensor")

    def in_order(own, other, dim):
        return jnp.where(
            side == 0,
            jnp.concatenate([own, other], axis=dim),
            jnp.concatenate([other, own], axis=dim),
        )

    own_blocks, blocks = [], []
    for group in range(groups):
        cols = slice(group * LANES, (group + 1) * LANES)
        weight = jnp.concatenate([key_weight[:, cols], value_weight[:, cols]], axis=1)
        shift = jnp.concatenate([jnp.zeros((LANES,), F32), value_shift[cols]])
        own_blocks.append((dot(tokens, weight, NN) + shift).astype(BF16))
    for own in own_blocks:
        across = flip(own, "dp", 1)
        blocks.append((own, flip(own, "dp", 0), across, flip(across, "dp", 0)))
    queries = (dot(tokens, query_weight, NN) + query_bias.reshape(local)).astype(BF16)
    out_whole = in_order(out_weight, flip(out_weight, "tensor", 0), 0)

    outs, own_context, other_context = [], [], []
    for group in range(groups):
        out, lse = attend(queries, group, blocks[group], scale)
        outs.append((out, lse))
        own_context.append(out.astype(BF16))
        other_context.append(flip(own_context[-1], "tensor", 0))
    context = jnp.concatenate(own_context, axis=1)
    context_whole = in_order(context, jnp.concatenate(other_context, axis=1), 1)

    step = rows // CHUNKS
    cuts = [slice(i * step, (i + 1) * step) for i in range(CHUNKS)]
    firsts, lows, actives, active_lows, feed_lows, feed_others = [], [], [], [], [], []
    done = context_whole
    for cut in cuts:
        attention = dot(after(context_whole[cut], done), out_whole, NN) + out_bias
        first = jax.vjp(
            layer_norm, tokens[cut].astype(F32) + attention, first_gain, first_shift
        )
        low = first[0].astype(BF16)
        hidden = dot(low, up_weight, NN) + up_bias.reshape(-1)
        active = jax.vjp(gelu_tanh, hidden)
        active_low = active[0].astype(BF16)
        feed_low = dot(active_low, down_weight, NN).astype(BF16)
        done = feed_low
        firsts.append(first)
        lows.append(low)
        actives.append(active)
        active_lows.append(active_low)
        feed_lows.append(feed_low)
        feed_others.append(flip(feed_low, "tensor", 0))
    seconds, second_grads, feed_grads, hidden_lows, grad_lows, grad_others = (
        [], [], [], [], [], [],
    )
    for i, cut in enumerate(cuts):
        other = after(feed_others[i], done)
        feed = feed_lows[i].astype(F32) + other.astype(F32) + down_bias
        second, second_back = jax.vjp(
            layer_norm, firsts[i][0] + feed, second_gain, second_shift
        )
        grads = second_back(cotangent[cut].astype(F32))
        feed_grad = grads[0].astype(BF16)
        hidden_low = actives[i][1](dot(feed_grad, down_weight, NT))[0].astype(BF16)
        grad_low = dot(hidden_low, up_weight, NT).astype(BF16)
        done = grad_low
        seconds.append(second.astype(BF16))
        second_grads.append(grads)
        feed_grads.append(feed_grad)
        hidden_lows.append(hidden_low)
        grad_lows.append(grad_low)
        grad_others.append(flip(grad_low, "tensor", 0))
    layer_output = jnp.concatenate(seconds, axis=0)
    feed_grad = after(jnp.concatenate(feed_grads, axis=0), done)
    active_low = jnp.concatenate(active_lows, axis=0)
    down_rows = dot(feed_grad, active_low, TN).astype(BF16)
    down_scatter = Scatter(down_rows, BF16)
    hidden_low = after(jnp.concatenate(hidden_lows, axis=0), down_rows)
    first_low = jnp.concatenate(lows, axis=0)
    up_rows = dot(first_low, hidden_low, TN).astype(BF16)
    up_scatter = Scatter(up_rows, BF16)
    downbias_grad = jnp.sum(feed_grad.astype(F32), axis=0)
    upbias_grad = jnp.sum(hidden_low.astype(F32), axis=0)
    secondgain_grad = sum(grads[1] for grads in second_grads)
    secondshift_grad = sum(grads[2] for grads in second_grads)
    done = down_scatter.land(up_rows)

    attention_backs, firstgain_parts, firstshift_parts = [], [], []
    for i in range(CHUNKS):
        other = after(grad_others[i], done)
        grad = second_grads[i][0] + (grad_lows[i].astype(F32) + other.astype(F32))
        grads = firsts[i][1](grad)
        attention_backs.append(grads[0])
        firstgain_parts.append(grads[1])
        firstshift_parts.append(grads[2])
    attention_back = jnp.concatenate(attention_backs, axis=0)
    firstgain_grad = sum(firstgain_parts)
    firstshift_grad = sum(firstshift_parts)
    attention_grad = attention_back.astype(BF16)
    outbias_grad = jnp.sum(attention_grad.astype(F32), axis=0)
    context_grad = dot(attention_grad, out_weight, NT).astype(BF16)
    out_rows = dot(attention_grad, context, TN).astype(BF16)
    out_scatter = Scatter(out_rows, BF16)

    query_grads, key_grads, value_grads = [], [], []
    flights, crossings = {}, {}

    def core_level(group, mark):
        own, across, beside, diagonal = flights.pop(group)
        beside, diagonal = after(beside, mark), after(diagonal, mark)
        here = own.astype(F32) + beside.astype(F32)
        there = (across.astype(F32) + diagonal.astype(F32)).astype(BF16)
        crossings[group] = (here, flip(there, "dp", 1))
        return there

    def chip_level(group, mark):
        here, there = crossings.pop(group)
        there = after(there, mark)
        total = (here + there.astype(F32)).astype(BF16)
        key_grads.append(total[:, :LANES])
        value_grads.append(total[:, LANES:])
        return total

    def launch_back(group, *earlier):
        out, lse = outs[group]
        query_part, own, beside, across, diagonal = attend_back(
            after(queries, *earlier), context_grad, group, out, lse, blocks[group], scale
        )
        query_grads.append(query_part)
        flights[group] = (own, across, flip(beside, "dp", 0), flip(diagonal, "dp", 0))
        return query_part

    mark = launch_back(0, up_scatter.land(out_rows))
    mark = launch_back(1, down_scatter.land(mark), out_scatter.land(mark))
    mark = launch_back(
        2,
        core_level(0, mark),
        up_scatter.land(mark),
        down_scatter.land(mark),
        out_scatter.land(mark),
    )
    mark = launch_back(
        3,
        core_level(1, mark),
        chip_level(0, mark),
        up_scatter.land(mark),
        down_scatter.land(mark),
        out_scatter.land(mark),
    )
    core_level(2, mark)
    core_level(3, mark)
    chip_level(1, mark)
    chip_level(2, mark)
    chip_level(3, mark)
    outweight_grad = out_scatter.result()
    upweight_grad = up_scatter.result()
    downweight_grad = down_scatter.result()
    joined_grads = jnp.concatenate(query_grads + key_grads + value_grads, axis=1)
    flat_proj = jnp.concatenate([query_weight, key_weight, value_weight], axis=1)
    proj_grad = Scatter(dot(tokens, joined_grads, TN).astype(BF16), BF16).result()
    bias_grads = jnp.sum(joined_grads.astype(F32), axis=0)
    tokens_grad = attention_back + pair_sum(dot(joined_grads, flat_proj, NT))

    size = lax.axis_size("dp")

    def by_dp(vector, leading):
        return (
            vector.reshape(leading, size, -1).transpose(1, 0, 2).reshape(size, -1)
        )

    units = up_bias.shape[0]
    small = [
        (by_dp(bias_grads[:local], heads), heads),
        (by_dp(bias_grads[2 * local :], heads), heads),
        (by_dp(outbias_grad, 1), 0),
        (by_dp(firstgain_grad, 1), 0),
        (by_dp(firstshift_grad, 1), 0),
        (by_dp(upbias_grad, units), units),
        (by_dp(downbias_grad, 1), 0),
        (by_dp(secondgain_grad, 1), 0),
        (by_dp(secondshift_grad, 1), 0),
    ]
    packed = Scatter(jnp.concatenate([part for part, _ in small], axis=1), F32).result()[0]
    vectors, at = [], 0
    for part, leading in small:
        piece = packed[at : at + part.shape[1]]
        at += part.shape[1]
        vectors.append(piece.reshape(leading, -1) if leading else piece)
    return (
        layer_output,
        tokens_grad,
        proj_grad.reshape(width // size, 3, local),
        vectors[0],
        vectors[1],
        outweight_grad.T,
        vectors[2],
        vectors[3],
        vectors[4],
        upweight_grad,
        vectors[5],
        downweight_grad.T,
        vectors[6],
        vectors[7],
        vectors[8],
    )


def solution(mesh):
    return jax.shard_map(
        body,
        mesh=mesh,
        in_specs=(
            P("dp", None),
            P(None, None, "tensor"),
            P("tensor", None),
            P("tensor", None),
            P("tensor", None),
            P(),
            P(),
            P(),
            P(None, "tensor"),
            P("tensor", None),
            P("tensor", None),
            P(),
            P(),
            P(),
            P("dp", None),
        ),
        out_specs=(
            P("dp", None),
            P("dp", None),
            P("dp", None, "tensor"),
            P("tensor", "dp"),
            P("tensor", "dp"),
            P("tensor", "dp"),
            P("dp"),
            P("dp"),
            P("dp"),
            P("dp", "tensor"),
            P("tensor", "dp"),
            P("tensor", "dp"),
            P("dp"),
            P("dp"),
            P("dp"),
        ),
        check_vma=False,
    )
```

```python
import functools
import math

import jax
import jax.numpy as jnp
from jax import lax
from jax.experimental import pallas as pl
from jax.experimental.pallas import tpu as pltpu
from jax.sharding import PartitionSpec as P

EPS = 1e-12
F32 = jnp.float32
BF16 = jnp.bfloat16
LANES = 128
HALF = 64
SOURCES = 4
CHUNKS = 2
NN = (((1,), (0,)), ((), ()))
NT = (((1,), (1,)), ((), ()))
TN = (((0,), (0,)), ((), ()))
MESH = pl.DeviceIdType.MESH


def dot(left, right, dims):
    return lax.dot_general(left, right, dims, preferred_element_type=F32)


def flip(value, axis, bit):
    pairs = [(source, source ^ (1 << bit)) for source in range(lax.axis_size(axis))]
    return lax.ppermute(value, axis, pairs)


def pair_sum(partial):
    low = partial.astype(BF16)
    return low.astype(F32) + flip(low, "tensor", 0).astype(F32)


def partner(axis, bit):
    place = lax.axis_index(axis)
    return {axis: place + (1 - 2 * (place // (1 << bit) % 2)) * (1 << bit)}


def greet(links):
    barrier = pltpu.get_barrier_semaphore()
    for axis, bit in links:
        pl.semaphore_signal(
            barrier, inc=1, device_id=partner(axis, bit), device_id_type=MESH
        )
    pl.semaphore_wait(barrier, len(links))


def send(source, target, semaphores, index, axis, bit):
    return pltpu.make_async_remote_copy(
        src_ref=source,
        dst_ref=target,
        send_sem=semaphores.at[0, index],
        recv_sem=semaphores.at[1, index],
        device_id=partner(axis, bit),
        device_id_type=MESH,
    )


def exchange_kernel(links, *refs):
    count = len(links)
    semaphores = refs[-1]
    greet(sorted(set(links)))
    copies = [
        send(refs[i], refs[count + i], semaphores, i, *links[i]) for i in range(count)
    ]
    for copy in copies:
        copy.start()
    for copy in copies:
        copy.wait()


def exchange(cargo, collective_id):
    links = [link for _, link in cargo]
    values = [value for value, _ in cargo]
    anywhere = pl.BlockSpec(memory_space=pl.ANY)
    return pl.pallas_call(
        functools.partial(exchange_kernel, links),
        in_specs=[anywhere] * len(values),
        out_specs=[anywhere] * len(values),
        out_shape=[jax.ShapeDtypeStruct(v.shape, v.dtype) for v in values],
        scratch_shapes=[pltpu.SemaphoreType.DMA((2, len(values)))],
        compiler_params=pltpu.CompilerParams(
            collective_id=collective_id, has_side_effects=True
        ),
        cost_estimate=pl.CostEstimate(
            flops=0, bytes_accessed=16 << 20, transcendentals=0
        ),
        name="exchange",
    )(*values)


def after(value, *earlier):
    return lax.optimization_barrier((value, earlier))[0]


class Scatter:
    def __init__(self, rows, wire, far_first=False):
        size = lax.axis_size("dp")
        bits = size.bit_length() - 1
        self.part = rows.shape[0] // size
        self.whole = rows
        self.wire = wire
        self.left = list(range(bits))[::-1]
        self.order = list(range(bits))
        if far_first and bits > 2:
            self.order = [0] + self.order[2:] + [1]
        self.split()

    def split(self, ready=None):
        self.cargo = None
        if not self.order:
            return
        bit = self.order.pop(0)
        high = 1 << self.left.index(bit)
        self.left.remove(bit)
        if ready is None:
            view = self.whole.reshape(high, 2, -1, self.whole.shape[-1])
            own = lax.axis_index("dp") >> bit & 1
            ready = [
                lax.dynamic_index_in_dim(view, side, 1, keepdims=False).reshape(
                    -1, view.shape[-1]
                )
                for side in (own, 1 - own)
            ]
        self.keep = ready[0]
        self.cargo = (ready[1].astype(self.wire), ("dp", bit))

    def land(self, arrived):
        self.whole = self.keep.astype(F32) + arrived.astype(F32)
        self.split()
        return self.whole

    def fly(self):
        value, (axis, bit) = self.cargo
        return flip(value, axis, bit)

    def result(self):
        return self.whole


class Columns(Scatter):
    def __init__(self, other, cols):
        self.part, self.wire = other.part, other.wire
        self.left, self.order = list(other.left), list(other.order)
        link = other.cargo[1]
        self.keep = other.keep[:, cols]
        self.cargo = (other.cargo[0][:, cols], link)


class Ready(Scatter):
    def __init__(self, keep, out, far_first):
        size = lax.axis_size("dp")
        bits = size.bit_length() - 1
        self.part = 2 * keep.shape[0] // size
        self.wire = out.dtype
        self.left = list(range(bits))[::-1]
        self.order = list(range(bits))
        if far_first and bits > 2:
            self.order = [0] + self.order[2:] + [1]
        self.split([keep, out])


def layer_norm(rows, gain, shift):
    mean = jnp.mean(rows, axis=-1, keepdims=True)
    centered = rows - mean
    spread = jnp.mean(centered * centered, axis=-1, keepdims=True)
    return centered * lax.rsqrt(spread + EPS) * gain + shift


def gelu_tanh(values):
    return jax.nn.gelu(values, approximate=True)


def head_lanes(shape, head):
    lane = lax.broadcasted_iota(jnp.int32, shape, 1)
    return (lane < HALF) if head == 0 else (lane >= HALF)


def forward_kernel(scale, tile, *refs):
    q_ref = refs[0]
    k_refs = refs[1 : 1 + SOURCES]
    v_refs = refs[1 + SOURCES : 1 + 2 * SOURCES]
    o_ref, lse_ref, s_ref, vt_ref = refs[1 + 2 * SOURCES :]
    span = k_refs[0].shape[0]

    @pl.when(pl.program_id(0) == 0)
    def _():
        for source in range(SOURCES):
            vt_ref[:LANES, source * span : (source + 1) * span] = jnp.transpose(
                v_refs[source][...]
            )
        vt_ref[LANES:, :] = jnp.ones((vt_ref.shape[0] - LANES, vt_ref.shape[1]), BF16)

    q = q_ref[...] * scale
    outs = []
    for head in range(2):
        own = head_lanes(q.shape, head)
        qt = jnp.transpose(jnp.where(own, q, jnp.zeros_like(q)))
        peak = None
        for source in range(SOURCES):
            for start in range(0, span, tile):
                scores = dot(k_refs[source][start : start + tile, :], qt, NN)
                base = source * span + start
                s_ref[head, base : base + tile, :] = scores
                top = jnp.max(scores, axis=0, keepdims=True)
                peak = top if peak is None else jnp.maximum(peak, top)
        total = None
        for start in range(0, SOURCES * span, tile):
            weights = jnp.exp(s_ref[head, start : start + tile, :] - peak).astype(BF16)
            part = dot(vt_ref[:, start : start + tile], weights, NN)
            total = part if total is None else total + part
        mass = total[LANES : LANES + 1, :]
        outs.append(total[head * HALF : (head + 1) * HALF, :] / mass)
        lse_ref[head, :] = (peak + jnp.log(mass))[0]
    o_ref[...] = jnp.transpose(jnp.concatenate(outs, 0))


def attend(queries, group, blocks, scale):
    rows = queries.shape[0]
    span = blocks[0].shape[0]
    tq = rows // 2
    keys = SOURCES * span
    return pl.pallas_call(
        functools.partial(forward_kernel, scale, span // 2),
        grid=(rows // tq,),
        in_specs=[pl.BlockSpec((tq, LANES), lambda i: (i, group))]
        + [pl.BlockSpec((span, LANES), lambda i: (0, 0))] * SOURCES
        + [pl.BlockSpec((span, LANES), lambda i: (0, 1))] * SOURCES,
        out_specs=[
            pl.BlockSpec((tq, LANES), lambda i: (i, 0)),
            pl.BlockSpec((2, tq), lambda i: (0, i)),
        ],
        out_shape=[
            jax.ShapeDtypeStruct((rows, LANES), F32),
            jax.ShapeDtypeStruct((2, rows), F32),
        ],
        scratch_shapes=[
            pltpu.VMEM((2, keys, tq), F32),
            pltpu.VMEM((LANES + 16, keys), BF16),
        ],
        compiler_params=pltpu.CompilerParams(vmem_limit_bytes=40 << 20),
        cost_estimate=pl.CostEstimate(
            flops=16 * rows * keys * LANES,
            bytes_accessed=4 * (keys + rows) * LANES + 4 * rows * LANES,
            transcendentals=2 * rows * keys,
        ),
        name="attend",
    )(queries, *blocks, *blocks)


def thirds(value):
    high = value.astype(BF16).astype(F32)
    rest = value - high
    middle = rest.astype(BF16).astype(F32)
    return high, middle, rest - middle


def backward_kernel(scale, tile, links, *refs):
    count = len(links)
    q_ref, g_ref, o_ref, lse_ref = refs[:4]
    k_refs = refs[4 : 4 + SOURCES]
    v_refs = refs[4 + SOURCES : 4 + 2 * SOURCES]
    tokens_ref = refs[4 + 2 * SOURCES]
    refs = refs[5 + 2 * SOURCES :]
    cargo_refs, refs = refs[:count], refs[count:]
    joined_ref, sums_ref, keep_ref, out_ref = refs[:4]
    landing_refs, refs = refs[4 : 4 + count], refs[4 + count :]
    qt_ref, gt_ref, dqt_ref, k_ref, v_ref, d_ref = refs[:6]
    diagonal_ref, cross_ref, beside_ref = refs[6:9]
    diagonal_in, cross_in, beside_in, product_ref, semaphores = refs[9:]
    step = pl.program_id(0)
    rows = q_ref.shape[0]
    span = k_ref.shape[0]
    own_links = [("dp", 0), ("dp", 1)]
    copies = [
        send(cargo_refs[i], landing_refs[i], semaphores, i, *links[i])
        for i in range(count)
    ]
    diagonal_copy = send(diagonal_ref, diagonal_in, semaphores, count, "dp", 0)
    cross_copy = send(cross_ref, cross_in, semaphores, count + 1, "dp", 1)
    beside_copy = send(beside_ref, beside_in, semaphores, count + 2, "dp", 0)

    @pl.when(step == 0)
    def _():
        greet(sorted(set(own_links + links)))
        for copy in copies:
            copy.start()
        q = q_ref[...] * scale
        g = g_ref[...]
        products = jnp.transpose(g.astype(F32) * o_ref[...])
        row = lax.broadcasted_iota(jnp.int32, (LANES, rows), 0)
        for head in range(2):
            own = head_lanes(q.shape, head)
            qt_ref[head, :LANES, :] = jnp.transpose(jnp.where(own, q, jnp.zeros_like(q)))
            gt_ref[head, :LANES, :] = jnp.transpose(jnp.where(own, g, jnp.zeros_like(g)))
            centre = jnp.sum(
                products[head * HALF : (head + 1) * HALF], axis=0, keepdims=True
            )
            for ref, value in (
                (qt_ref, -lse_ref[head : head + 1, :]),
                (gt_ref, -centre),
            ):
                high, middle, low = thirds(value)
                ref[head, LANES:, :] = jnp.where(
                    row == 0,
                    high,
                    jnp.where(row == 1, middle, jnp.where(row == 2, low, 0.0)),
                ).astype(BF16)
        dqt_ref[...] = jnp.zeros_like(dqt_ref)

    @pl.when(step == 1)
    def _():
        diagonal_copy.start()

    @pl.when(step == 2)
    def _():
        cross_copy.start()

    @pl.when(step == 3)
    def _():
        beside_copy.start()

    for source in range(SOURCES):

        @pl.when(step == SOURCES - 1 - source)
        def _():
            k_ref[...] = k_refs[source][...]
            v_ref[...] = v_refs[source][...]

    for start in range(0, span, tile):
        k = k_ref[start : start + tile, :]
        v = v_ref[start : start + tile, :]
        one = jnp.ones_like(k)
        k_wide = jnp.concatenate([k, one], 1)
        v_wide = jnp.concatenate([v, one], 1)
        kt = jnp.transpose(k)
        parts = []
        for head in range(2):
            probs = jnp.exp(dot(k_wide, qt_ref[head], NN))
            centred = dot(v_wide, gt_ref[head], NN)
            score_grad = (probs * centred).astype(BF16)
            parts.append(
                (
                    dot(score_grad, q_ref[...], NN),
                    dot(probs.astype(BF16), g_ref[...], NN),
                )
            )
            dqt_ref[head * HALF : (head + 1) * HALF, :] += dot(
                kt[head * HALF : (head + 1) * HALF, :], score_grad, NN
            )
        first = head_lanes(k.shape, 0)
        d_ref[start : start + tile, :LANES] = (
            jnp.where(first, parts[0][0], parts[1][0]) * scale
        ).astype(BF16)
        d_ref[start : start + tile, LANES:] = jnp.where(
            first, parts[0][1], parts[1][1]
        ).astype(BF16)

    @pl.when(step == 0)
    def _():
        diagonal_ref[...] = d_ref[...]

    @pl.when(step == 1)
    def _():
        diagonal_copy.wait()
        cross_ref[...] = (
            d_ref[...].astype(F32) + diagonal_in[...].astype(F32)
        ).astype(BF16)

    @pl.when(step == 2)
    def _():
        beside_ref[...] = d_ref[...]

    @pl.when(step == 3)
    def _():
        joined_ref[:, :LANES] = (jnp.transpose(dqt_ref[...]) * scale).astype(BF16)
        beside_copy.wait()
        cross_copy.wait()
        joined_ref[:, LANES:] = (
            d_ref[...].astype(F32)
            + beside_in[...].astype(F32)
            + cross_in[...].astype(F32)
        ).astype(BF16)
        joined = joined_ref[...]
        sums_ref[...] = jnp.sum(joined.astype(F32), axis=0, keepdims=True)
        pairs, _, part, _ = product_ref.shape
        for pair in range(0, pairs, 2):
            band = tokens_ref[2 * pair * part : 2 * (pair + 2) * part, :]
            product_ref[pair : pair + 2] = (
                dot(band, joined, NN).astype(BF16).reshape(2, 2, part, 3 * LANES)
            )
        side = lax.axis_index("dp") % 2
        keep_ref[...] = product_ref[:, side].reshape(keep_ref.shape)
        out_ref[...] = product_ref[:, 1 - side].reshape(out_ref.shape)
        for copy in copies:
            copy.wait()


def attend_back(
    queries, grads, tokens, group, context, lse, blocks, scale, cargo, collective_id
):
    rows = queries.shape[0]
    span = blocks[0].shape[0]
    keys = SOURCES * span
    size, width = lax.axis_size("dp"), tokens.shape[0]
    whole = lambda i: (0, 0)
    links = [link for _, link in cargo]
    values = [value for value, _ in cargo]
    anywhere = pl.BlockSpec(memory_space=pl.ANY)
    return pl.pallas_call(
        functools.partial(backward_kernel, scale, span // 2, links),
        grid=(SOURCES,),
        in_specs=[
            pl.BlockSpec((rows, LANES), lambda i: (0, group)),
            pl.BlockSpec((rows, LANES), lambda i: (0, group)),
            pl.BlockSpec((rows, LANES), whole),
            pl.BlockSpec((2, rows), whole),
        ]
        + [pl.BlockSpec((span, LANES), whole)] * SOURCES
        + [pl.BlockSpec((span, LANES), lambda i: (0, 1))] * SOURCES
        + [pl.BlockSpec(tokens.shape, whole)]
        + [anywhere] * len(values),
        out_specs=[
            pl.BlockSpec((rows, 3 * LANES), whole),
            pl.BlockSpec((1, 3 * LANES), whole),
            pl.BlockSpec((width // 2, 3 * LANES), whole),
            pl.BlockSpec((width // 2, 3 * LANES), whole),
        ]
        + [anywhere] * len(values),
        out_shape=[
            jax.ShapeDtypeStruct((rows, 3 * LANES), BF16),
            jax.ShapeDtypeStruct((1, 3 * LANES), F32),
            jax.ShapeDtypeStruct((width // 2, 3 * LANES), BF16),
            jax.ShapeDtypeStruct((width // 2, 3 * LANES), BF16),
        ]
        + [jax.ShapeDtypeStruct(v.shape, v.dtype) for v in values],
        scratch_shapes=[
            pltpu.VMEM((2, 2 * LANES, rows), BF16),
            pltpu.VMEM((2, 2 * LANES, rows), BF16),
            pltpu.VMEM((LANES, rows), F32),
            pltpu.VMEM((span, LANES), BF16),
            pltpu.VMEM((span, LANES), BF16),
        ]
        + [pltpu.VMEM((span, 2 * LANES), BF16)] * 7
        + [pltpu.VMEM((size // 2, 2, width // size, 3 * LANES), BF16)]
        + [pltpu.SemaphoreType.DMA((2, len(values) + 3))],
        compiler_params=pltpu.CompilerParams(
            vmem_limit_bytes=60 << 20,
            collective_id=collective_id,
            has_side_effects=True,
        ),
        cost_estimate=pl.CostEstimate(
            flops=28 * rows * keys * LANES,
            bytes_accessed=8 * keys * LANES + 12 * rows * LANES,
            transcendentals=2 * rows * keys,
        ),
        name="attend_back",
    )(queries, grads, context, lse, *blocks, *blocks, tokens, *values)


def merge_kernel(count, *refs):
    sides = []
    for base in (0, 3 * count):
        total = None
        for group in range(count):
            rows = refs[base + group]
            first, second = refs[base + count + 2 * group : base + count + 2 * group + 2]
            for value in (
                dot(rows[:, :LANES], first[...], NT),
                dot(rows[:, LANES:], second[...], NT),
            ):
                total = value if total is None else total + value
        sides.append(total)
    result = sides[0] + sides[1]
    for ref in refs[6 * count : -1]:
        result = result + ref[...]
    refs[-1][...] = result


def merge(own, own_weights, other, other_weights, *extra):
    count = len(own)
    rows, width = own[0].shape[0], own_weights[0].shape[0]
    tile = rows // 4
    row_spec = pl.BlockSpec((tile, 3 * LANES), lambda i: (i, 0))
    sum_spec = pl.BlockSpec((tile, width), lambda i: (i, 0))
    weight_specs = [
        pl.BlockSpec((width, LANES), lambda i: (0, 0)),
        pl.BlockSpec((width, 2 * LANES), lambda i: (0, 0)),
    ] * count
    return pl.pallas_call(
        functools.partial(merge_kernel, count),
        grid=(rows // tile,),
        in_specs=([row_spec] * count + weight_specs) * 2 + [sum_spec] * len(extra),
        out_specs=sum_spec,
        out_shape=jax.ShapeDtypeStruct((rows, width), F32),
        compiler_params=pltpu.CompilerParams(vmem_limit_bytes=48 << 20),
        cost_estimate=pl.CostEstimate(
            flops=12 * count * rows * width * LANES,
            bytes_accessed=8 * rows * width,
            transcendentals=0,
        ),
        name="merge",
    )(*own, *own_weights, *other, *other_weights, *extra)


def body(
    tokens,
    proj_weight,
    query_bias,
    value_bias,
    out_weight,
    out_bias,
    first_gain,
    first_shift,
    up_weight,
    up_bias,
    down_weight,
    down_bias,
    second_gain,
    second_shift,
    cotangent,
):
    rows, width = tokens.shape
    heads, head_size = query_bias.shape
    local = heads * head_size
    groups = local // LANES
    scale = 1.0 / math.sqrt(head_size)
    query_weight = proj_weight[:, 0, :]
    key_weight = proj_weight[:, 1, :]
    value_weight = proj_weight[:, 2, :]
    value_shift = value_bias.reshape(local)

    side = lax.axis_index("tensor")

    def in_order(own, other, dim):
        return jnp.where(
            side == 0,
            jnp.concatenate([own, other], axis=dim),
            jnp.concatenate([other, own], axis=dim),
        )

    own_blocks, blocks, weights = [], [], []
    for group in range(groups):
        cols = slice(group * LANES, (group + 1) * LANES)
        weight = jnp.concatenate([key_weight[:, cols], value_weight[:, cols]], axis=1)
        weights.append((query_weight[:, cols], weight))
        shift = jnp.concatenate([jnp.zeros((LANES,), F32), value_shift[cols]])
        own_blocks.append((dot(tokens, weight, NN) + shift).astype(BF16))
    for own in own_blocks:
        across = flip(own, "dp", 1)
        blocks.append((own, flip(own, "dp", 0), across, flip(across, "dp", 0)))
    queries = (dot(tokens, query_weight, NN) + query_bias.reshape(local)).astype(BF16)
    out_whole = in_order(out_weight, flip(out_weight, "tensor", 0), 0)

    outs, own_context, other_context = [], [], []
    across = ("tensor", 0)
    last_weights = [flip(part, "tensor", 0) for part in weights[-1]]
    for group in range(groups):
        if group == groups - 1:
            queries = after(queries, out_whole, *last_weights)
        out, lse = attend(queries, group, blocks[group], scale)
        outs.append((out, lse))
        own_context.append(out.astype(BF16))
        other_context.append(flip(own_context[-1], "tensor", 0))
    context = jnp.concatenate(own_context, axis=1)
    context_whole = in_order(context, jnp.concatenate(other_context, axis=1), 1)

    step = rows // CHUNKS
    cuts = [slice(i * step, (i + 1) * step) for i in range(CHUNKS)]
    firsts, lows, actives, active_lows, feed_lows, feed_others = [], [], [], [], [], []
    done = context_whole
    for cut in cuts:
        attention = dot(after(context_whole[cut], done), out_whole, NN) + out_bias
        first = jax.vjp(
            layer_norm, tokens[cut].astype(F32) + attention, first_gain, first_shift
        )
        low = first[0].astype(BF16)
        hidden = dot(low, up_weight, NN) + up_bias.reshape(-1)
        active = jax.vjp(gelu_tanh, hidden)
        active_low = active[0].astype(BF16)
        feed_low = dot(active_low, down_weight, NN).astype(BF16)
        done = feed_low
        firsts.append(first)
        lows.append(low)
        actives.append(active)
        active_lows.append(active_low)
        feed_lows.append(feed_low)
        feed_others.append(flip(feed_low, "tensor", 0))
    seconds, second_grads, feed_grads, hidden_lows, grad_lows, grad_others = (
        [], [], [], [], [], [],
    )
    for i, cut in enumerate(cuts):
        other = after(feed_others[i], done)
        feed = feed_lows[i].astype(F32) + other.astype(F32) + down_bias
        second, second_back = jax.vjp(
            layer_norm, firsts[i][0] + feed, second_gain, second_shift
        )
        grads = second_back(cotangent[cut].astype(F32))
        feed_grad = grads[0].astype(BF16)
        hidden_low = actives[i][1](dot(feed_grad, down_weight, NT))[0].astype(BF16)
        grad_low = dot(hidden_low, up_weight, NT).astype(BF16)
        done = grad_low
        seconds.append(second.astype(BF16))
        second_grads.append(grads)
        feed_grads.append(feed_grad)
        hidden_lows.append(hidden_low)
        grad_lows.append(grad_low)
        grad_others.append(flip(grad_low, "tensor", 0))
    layer_output = jnp.concatenate(seconds, axis=0)
    feed_grad = after(jnp.concatenate(feed_grads, axis=0), done)
    active_low = jnp.concatenate(active_lows, axis=0)
    down_rows = dot(feed_grad, active_low, TN).astype(BF16)
    down_scatter = Scatter(down_rows, BF16)
    down_flight = down_scatter.fly()
    hidden_low = after(jnp.concatenate(hidden_lows, axis=0), down_rows)
    first_low = jnp.concatenate(lows, axis=0)
    up_rows = dot(first_low, hidden_low, TN).astype(BF16)
    up_scatter = Scatter(up_rows, BF16, True)
    up_flight = up_scatter.fly()
    downbias_grad = jnp.sum(feed_grad.astype(F32), axis=0)
    upbias_grad = jnp.sum(hidden_low.astype(F32), axis=0)
    secondgain_grad = sum(grads[1] for grads in second_grads)
    secondshift_grad = sum(grads[2] for grads in second_grads)
    done = down_scatter.land(after(down_flight, up_rows))
    middle = down_rows.shape[1] // 2
    down_parts = [
        Columns(down_scatter, slice(None, middle)),
        Columns(down_scatter, slice(middle, None)),
    ]

    attention_backs, firstgain_parts, firstshift_parts = [], [], []
    for i in range(CHUNKS):
        other = after(grad_others[i], done)
        grad = second_grads[i][0] + (grad_lows[i].astype(F32) + other.astype(F32))
        grads = firsts[i][1](grad)
        attention_backs.append(grads[0])
        firstgain_parts.append(grads[1])
        firstshift_parts.append(grads[2])
    attention_back = jnp.concatenate(attention_backs, axis=0)
    firstgain_grad = sum(firstgain_parts)
    firstshift_grad = sum(firstshift_parts)
    attention_grad = attention_back.astype(BF16)
    outbias_grad = jnp.sum(attention_grad.astype(F32), axis=0)
    context_grad = dot(attention_grad, out_weight, NT).astype(BF16)
    out_rows = dot(attention_grad, context, TN).astype(BF16)
    out_scatter = Scatter(out_rows, BF16)
    up_scatter.land(after(up_flight, out_rows))

    size = lax.axis_size("dp")

    def by_dp(vector, leading):
        return (
            vector.reshape(leading, size, -1).transpose(1, 0, 2).reshape(size, -1)
        )

    def unpack(packed, pieces):
        vectors, at = [], 0
        for part, leading in pieces:
            piece = packed[at : at + part.shape[1]]
            at += part.shape[1]
            vectors.append(piece.reshape(leading, -1) if leading else piece)
        return vectors

    units = up_bias.shape[0]
    early = [
        (by_dp(outbias_grad, 1), 0),
        (by_dp(firstgain_grad, 1), 0),
        (by_dp(firstshift_grad, 1), 0),
        (by_dp(upbias_grad, units), units),
        (by_dp(downbias_grad, 1), 0),
        (by_dp(secondgain_grad, 1), 0),
        (by_dp(secondshift_grad, 1), 0),
    ]
    early_scatter = Scatter(jnp.concatenate([part for part, _ in early], axis=1), F32)

    tokens_turned = tokens.T
    trips = [[] for _ in range(groups)]
    for group in range(groups - 1):
        query_trip = group if group == 0 else min(group, groups - 1)
        pair_trip = max(0, group - 1) if group < groups - 2 else groups - 1
        trips[query_trip].append((group, 0))
        trips[pair_trip].append((group, 1))
    other_weights = [[None, None] for _ in range(groups - 1)] + [last_weights]
    joined, others, sums, proj_scatters = [], [], [], []
    active = [up_scatter, out_scatter, early_scatter, down_parts[0]]
    for group in range(groups):
        cargo = [scatter.cargo for scatter in active]
        cargo += [(weights[place][piece], across) for place, piece in trips[group]]
        if group > 0:
            cargo.append((joined[-1], across))
        out, lse = outs[group]
        rows_back, row_sums, keep, outgoing, *arrived = attend_back(
            queries,
            context_grad,
            tokens_turned,
            group,
            out,
            lse,
            blocks[group],
            scale,
            cargo,
            group,
        )
        for scatter in active:
            scatter.land(arrived.pop(0))
        for place, piece in trips[group]:
            other_weights[place][piece] = arrived.pop(0)
        if group > 0:
            others.append(arrived.pop(0))
        joined.append(rows_back)
        sums.append(row_sums.reshape(3, LANES))
        proj_scatters.append(Ready(keep, outgoing, group < groups - 1))
        active.append(proj_scatters[-1])
        if group == 0:
            active.append(down_parts[1])
        active = [scatter for scatter in active if scatter.cargo is not None]
    sums = jnp.stack(sums, axis=1).reshape(3, local)
    late = [(by_dp(sums[0], heads), heads), (by_dp(sums[2], heads), heads)]
    late_scatter = Scatter(jnp.concatenate([part for part, _ in late], axis=1), F32)
    active.append(late_scatter)
    others.append(flip(joined[-1], "tensor", 0))

    def spread(parts):
        return [piece for pair in parts for piece in pair]

    partial = merge(
        joined[:-1], spread(weights[:-1]), others[:-1], spread(other_weights[:-1])
    )
    stage = groups
    while active:
        arrived = exchange([scatter.cargo for scatter in active], stage)
        stage += 1
        for scatter, value in zip(active, arrived):
            scatter.land(value)
        active = [scatter for scatter in active if scatter.cargo is not None]
    tokens_grad = merge(
        joined[-1:],
        spread(weights[-1:]),
        others[-1:],
        spread(other_weights[-1:]),
        partial,
        attention_back,
    )
    outweight_grad = out_scatter.result()
    upweight_grad = up_scatter.result()
    downweight_grad = jnp.concatenate([part.result() for part in down_parts], axis=1)
    proj_grad = jnp.stack(
        [scatter.result().reshape(-1, 3, LANES) for scatter in proj_scatters], axis=2
    )
    vectors = unpack(late_scatter.result()[0], late) + unpack(
        early_scatter.result()[0], early
    )
    return (
        layer_output,
        tokens_grad,
        proj_grad.reshape(width // size, 3, local),
        vectors[0],
        vectors[1],
        outweight_grad.T,
        vectors[2],
        vectors[3],
        vectors[4],
        upweight_grad,
        vectors[5],
        downweight_grad.T,
        vectors[6],
        vectors[7],
        vectors[8],
    )


def solution(mesh):
    return jax.shard_map(
        body,
        mesh=mesh,
        in_specs=(
            P("dp", None),
            P(None, None, "tensor"),
            P("tensor", None),
            P("tensor", None),
            P("tensor", None),
            P(),
            P(),
            P(),
            P(None, "tensor"),
            P("tensor", None),
            P("tensor", None),
            P(),
            P(),
            P(),
            P("dp", None),
        ),
        out_specs=(
            P("dp", None),
            P("dp", None),
            P("dp", None, "tensor"),
            P("tensor", "dp"),
            P("tensor", "dp"),
            P("tensor", "dp"),
            P("dp"),
            P("dp"),
            P("dp"),
            P("dp", "tensor"),
            P("tensor", "dp"),
            P("tensor", "dp"),
            P("dp"),
            P("dp"),
            P("dp"),
        ),
        check_vma=False,
    )
```

```python
import functools
import math

import jax
import jax.numpy as jnp
from jax import lax
from jax.experimental import pallas as pl
from jax.experimental.pallas import tpu as pltpu
from jax.sharding import PartitionSpec as P

EPS = 1e-12
F32 = jnp.float32
BF16 = jnp.bfloat16
LANES = 128
HALF = 64
SOURCES = 4
CHUNKS = 2
NN = (((1,), (0,)), ((), ()))
NT = (((1,), (1,)), ((), ()))
TN = (((0,), (0,)), ((), ()))
MESH = pl.DeviceIdType.MESH


def dot(left, right, dims):
    return lax.dot_general(left, right, dims, preferred_element_type=F32)


def flip(value, axis, bit):
    pairs = [(source, source ^ (1 << bit)) for source in range(lax.axis_size(axis))]
    return lax.ppermute(value, axis, pairs)


def pair_sum(partial):
    low = partial.astype(BF16)
    return low.astype(F32) + flip(low, "tensor", 0).astype(F32)


def partner(axis, bit):
    place = lax.axis_index(axis)
    return {axis: place + (1 - 2 * (place // (1 << bit) % 2)) * (1 << bit)}


def greet(links):
    barrier = pltpu.get_barrier_semaphore()
    for axis, bit in links:
        pl.semaphore_signal(
            barrier, inc=1, device_id=partner(axis, bit), device_id_type=MESH
        )
    pl.semaphore_wait(barrier, len(links))


def send(source, target, semaphores, index, axis, bit):
    return pltpu.make_async_remote_copy(
        src_ref=source,
        dst_ref=target,
        send_sem=semaphores.at[0, index],
        recv_sem=semaphores.at[1, index],
        device_id=partner(axis, bit),
        device_id_type=MESH,
    )


def after(value, *earlier):
    return lax.optimization_barrier((value, earlier))[0]


def sides(value, bit, left):
    view = value.reshape(1 << left.index(bit), 2, -1, value.shape[-1])
    own = lax.axis_index("dp") >> bit & 1
    return [
        lax.dynamic_index_in_dim(view, side, 1, keepdims=False).reshape(
            -1, view.shape[-1]
        )
        for side in (own, 1 - own)
    ]


class Scatter:
    def __init__(self, rows, wire, far_first=False):
        size = lax.axis_size("dp")
        bits = size.bit_length() - 1
        self.part = rows.shape[0] // size
        self.whole = rows
        self.wire = wire
        self.left = list(range(bits))[::-1]
        self.order = list(range(bits))
        if far_first and bits > 2:
            self.order = [0] + self.order[2:] + [1]
        self.split()

    def split(self, ready=None):
        self.cargo = None
        if not self.order:
            return
        bit = self.order.pop(0)
        if ready is None:
            ready = sides(self.whole, bit, self.left)
        self.left.remove(bit)
        self.keep = ready[0]
        self.cargo = (ready[1].astype(self.wire), ("dp", bit))

    def gather(self, arrived):
        self.whole = self.keep.astype(F32) + arrived.astype(F32)
        return self.whole

    def land(self, arrived):
        if not self.order:
            self.cargo = None
            return self.gather(arrived)
        bit = self.order[0]
        kept, sent = sides(self.keep, bit, self.left), sides(arrived, bit, self.left)
        self.split([a.astype(F32) + b.astype(F32) for a, b in zip(kept, sent)])

    def fly(self):
        value, (axis, bit) = self.cargo
        return flip(value, axis, bit)

    def result(self):
        return self.whole


class Columns(Scatter):
    def __init__(self, other, cols, far_first=False):
        self.part, self.wire = other.part, other.wire
        self.left, self.order = list(other.left), list(other.order)
        if far_first and len(self.order) > 1:
            self.order = self.order[1:] + self.order[:1]
        self.whole = other.whole[:, cols]
        self.split()


class Ready(Scatter):
    def __init__(self, keep, out, far_first):
        size = lax.axis_size("dp")
        bits = size.bit_length() - 1
        self.part = 2 * keep.shape[0] // size
        self.wire = out.dtype
        self.left = list(range(bits))[::-1]
        self.order = list(range(bits))
        if far_first and bits > 2:
            self.order = [0] + self.order[2:] + [1]
        self.split([keep, out])


def layer_norm(rows, gain, shift):
    mean = jnp.mean(rows, axis=-1, keepdims=True)
    centered = rows - mean
    spread = jnp.mean(centered * centered, axis=-1, keepdims=True)
    return centered * lax.rsqrt(spread + EPS) * gain + shift


def gelu_tanh(values):
    return jax.nn.gelu(values, approximate=True)


def head_lanes(shape, head):
    lane = lax.broadcasted_iota(jnp.int32, shape, 1)
    return (lane < HALF) if head == 0 else (lane >= HALF)


def forward_kernel(scale, tile, *refs):
    q_ref = refs[0]
    k_refs = refs[1 : 1 + SOURCES]
    v_refs = refs[1 + SOURCES : 1 + 2 * SOURCES]
    o_ref, lse_ref, s_ref, vt_ref = refs[1 + 2 * SOURCES :]
    span = k_refs[0].shape[0]

    @pl.when(pl.program_id(0) == 0)
    def _():
        for source in range(SOURCES):
            vt_ref[:LANES, source * span : (source + 1) * span] = jnp.transpose(
                v_refs[source][...]
            )
        vt_ref[LANES:, :] = jnp.ones((vt_ref.shape[0] - LANES, vt_ref.shape[1]), BF16)

    q = q_ref[...] * scale
    outs = []
    for head in range(2):
        own = head_lanes(q.shape, head)
        qt = jnp.transpose(jnp.where(own, q, jnp.zeros_like(q)))
        peak = None
        for source in range(SOURCES):
            for start in range(0, span, tile):
                scores = dot(k_refs[source][start : start + tile, :], qt, NN)
                base = source * span + start
                s_ref[head, base : base + tile, :] = scores
                top = jnp.max(scores, axis=0, keepdims=True)
                peak = top if peak is None else jnp.maximum(peak, top)
        total = None
        for start in range(0, SOURCES * span, tile):
            weights = jnp.exp(s_ref[head, start : start + tile, :] - peak).astype(BF16)
            part = dot(vt_ref[:, start : start + tile], weights, NN)
            total = part if total is None else total + part
        mass = total[LANES : LANES + 1, :]
        outs.append(total[head * HALF : (head + 1) * HALF, :] / mass)
        lse_ref[head, :] = (peak + jnp.log(mass))[0]
    o_ref[...] = jnp.transpose(jnp.concatenate(outs, 0))


def attend(queries, group, blocks, scale):
    rows = queries.shape[0]
    span = blocks[0].shape[0]
    tq = rows // 2
    keys = SOURCES * span
    return pl.pallas_call(
        functools.partial(forward_kernel, scale, span // 2),
        grid=(rows // tq,),
        in_specs=[pl.BlockSpec((tq, LANES), lambda i: (i, group))]
        + [pl.BlockSpec((span, LANES), lambda i: (0, 0))] * SOURCES
        + [pl.BlockSpec((span, LANES), lambda i: (0, 1))] * SOURCES,
        out_specs=[
            pl.BlockSpec((tq, LANES), lambda i: (i, 0)),
            pl.BlockSpec((2, tq), lambda i: (0, i)),
        ],
        out_shape=[
            jax.ShapeDtypeStruct((rows, LANES), F32),
            jax.ShapeDtypeStruct((2, rows), F32),
        ],
        scratch_shapes=[
            pltpu.VMEM((2, keys, tq), F32),
            pltpu.VMEM((LANES + 16, keys), BF16),
        ],
        compiler_params=pltpu.CompilerParams(vmem_limit_bytes=40 << 20),
        cost_estimate=pl.CostEstimate(
            flops=16 * rows * keys * LANES,
            bytes_accessed=4 * (keys + rows) * LANES + 4 * rows * LANES,
            transcendentals=2 * rows * keys,
        ),
        name="attend",
    )(queries, *blocks, *blocks)


def thirds(value):
    high = value.astype(BF16).astype(F32)
    rest = value - high
    middle = rest.astype(BF16).astype(F32)
    return high, middle, rest - middle


def backward_kernel(scale, tile, links, *refs):
    count = len(links)
    q_ref, g_ref, o_ref, lse_ref = refs[:4]
    k_refs = refs[4 : 4 + SOURCES]
    v_refs = refs[4 + SOURCES : 4 + 2 * SOURCES]
    tokens_ref = refs[4 + 2 * SOURCES]
    refs = refs[5 + 2 * SOURCES :]
    cargo_refs, refs = refs[:count], refs[count:]
    joined_ref, sums_ref, keep_ref, out_ref = refs[:4]
    landing_refs, refs = refs[4 : 4 + count], refs[4 + count :]
    qt_ref, gt_ref, dqt_ref, k_ref, v_ref, d_ref = refs[:6]
    diagonal_ref, cross_ref, beside_ref = refs[6:9]
    diagonal_in, cross_in, beside_in, product_ref, turned_ref, semaphores, local = refs[9:]
    turned_copy = pltpu.make_async_copy(tokens_ref, turned_ref, local.at[0])
    step = pl.program_id(0)
    rows = q_ref.shape[0]
    own_links = [("dp", 0), ("dp", 1)]
    copies = [
        send(cargo_refs[i], landing_refs[i], semaphores, i, *links[i])
        for i in range(count)
    ]
    halves = [slice(half * tile, (half + 1) * tile) for half in range(2)]

    def part_copies(source, target, first, bit):
        return [
            send(source.at[rows], target.at[rows], semaphores, count + first + i, "dp", bit)
            for i, rows in enumerate(halves)
        ]

    diagonal_copies = part_copies(diagonal_ref, diagonal_in, 0, 0)
    cross_copies = part_copies(cross_ref, cross_in, 2, 1)
    beside_copies = part_copies(beside_ref, beside_in, 4, 0)

    @pl.when(step == 0)
    def _():
        greet(sorted(set(own_links + links)))
        for copy in copies:
            copy.start()
        turned_copy.start()
        q = q_ref[...] * scale
        g = g_ref[...]
        products = jnp.transpose(g.astype(F32) * o_ref[...])
        row = lax.broadcasted_iota(jnp.int32, (LANES, rows), 0)
        for head in range(2):
            own = head_lanes(q.shape, head)
            qt_ref[head, :LANES, :] = jnp.transpose(jnp.where(own, q, jnp.zeros_like(q)))
            gt_ref[head, :LANES, :] = jnp.transpose(jnp.where(own, g, jnp.zeros_like(g)))
            centre = jnp.sum(
                products[head * HALF : (head + 1) * HALF], axis=0, keepdims=True
            )
            for ref, value in (
                (qt_ref, -lse_ref[head : head + 1, :]),
                (gt_ref, -centre),
            ):
                high, middle, low = thirds(value)
                ref[head, LANES:, :] = jnp.where(
                    row == 0,
                    high,
                    jnp.where(row == 1, middle, jnp.where(row == 2, low, 0.0)),
                ).astype(BF16)
        dqt_ref[...] = jnp.zeros_like(dqt_ref)

    for first, later in ((1, diagonal_copies), (3, cross_copies), (5, beside_copies)):
        for half in range(2):

            @pl.when(step == first + half)
            def _():
                later[half].start()

    for source in range(SOURCES):
        for half in range(2):

            @pl.when(step == 2 * (SOURCES - 1 - source) + half)
            def _():
                k_ref[...] = k_refs[source][halves[half], :]
                v_ref[...] = v_refs[source][halves[half], :]

    k = k_ref[...]
    v = v_ref[...]
    one = jnp.ones_like(k)
    k_wide = jnp.concatenate([k, one], 1)
    v_wide = jnp.concatenate([v, one], 1)
    kt = jnp.transpose(k)
    parts = []
    for head in range(2):
        probs = jnp.exp(dot(k_wide, qt_ref[head], NN))
        centred = dot(v_wide, gt_ref[head], NN)
        score_grad = (probs * centred).astype(BF16)
        parts.append(
            (
                dot(score_grad, q_ref[...], NN),
                dot(probs.astype(BF16), g_ref[...], NN),
            )
        )
        dqt_ref[head * HALF : (head + 1) * HALF, :] += dot(
            kt[head * HALF : (head + 1) * HALF, :], score_grad, NN
        )
    first = head_lanes(k.shape, 0)
    d_ref[:, :LANES] = (jnp.where(first, parts[0][0], parts[1][0]) * scale).astype(BF16)
    d_ref[:, LANES:] = jnp.where(first, parts[0][1], parts[1][1]).astype(BF16)

    for half in range(2):
        band = halves[half]

        @pl.when(step == half)
        def _():
            diagonal_ref[band, :] = d_ref[...]

        @pl.when(step == 2 + half)
        def _():
            diagonal_copies[half].wait()
            cross_ref[band, :] = (
                d_ref[...].astype(F32) + diagonal_in[band, :].astype(F32)
            ).astype(BF16)

        @pl.when(step == 4 + half)
        def _():
            beside_ref[band, :] = d_ref[...]

        @pl.when(step == 6 + half)
        def _():
            beside_copies[half].wait()
            cross_copies[half].wait()
            joined_ref[band, LANES:] = (
                d_ref[...].astype(F32)
                + beside_in[band, :].astype(F32)
                + cross_in[band, :].astype(F32)
            ).astype(BF16)

    @pl.when(step == 7)
    def _():
        joined_ref[:, :LANES] = (jnp.transpose(dqt_ref[...]) * scale).astype(BF16)
        joined = joined_ref[...]
        sums_ref[...] = jnp.sum(joined.astype(F32), axis=0, keepdims=True)
        turned_copy.wait()
        pairs, _, part, _ = product_ref.shape
        for pair in range(0, pairs, 2):
            band = turned_ref[2 * pair * part : 2 * (pair + 2) * part, :]
            product_ref[pair : pair + 2] = (
                dot(band, joined, NN).astype(BF16).reshape(2, 2, part, 3 * LANES)
            )
        side = lax.axis_index("dp") % 2
        keep_ref[...] = product_ref[:, side].reshape(keep_ref.shape)
        out_ref[...] = product_ref[:, 1 - side].reshape(out_ref.shape)
        for copy in copies:
            copy.wait()


def attend_back(
    queries, grads, tokens, group, context, lse, blocks, scale, cargo, collective_id
):
    rows = queries.shape[0]
    span = blocks[0].shape[0]
    keys = SOURCES * span
    size, width = lax.axis_size("dp"), tokens.shape[0]
    whole = lambda i: (0, 0)
    links = [link for _, link in cargo]
    values = [value for value, _ in cargo]
    anywhere = pl.BlockSpec(memory_space=pl.ANY)
    return pl.pallas_call(
        functools.partial(backward_kernel, scale, span // 2, links),
        grid=(2 * SOURCES,),
        in_specs=[
            pl.BlockSpec((rows, LANES), lambda i: (0, group)),
            pl.BlockSpec((rows, LANES), lambda i: (0, group)),
            pl.BlockSpec((rows, LANES), whole),
            pl.BlockSpec((2, rows), whole),
        ]
        + [pl.BlockSpec((span, LANES), whole)] * SOURCES
        + [pl.BlockSpec((span, LANES), lambda i: (0, 1))] * SOURCES
        + [anywhere] * (1 + len(values)),
        out_specs=[
            pl.BlockSpec((rows, 3 * LANES), whole),
            pl.BlockSpec((1, 3 * LANES), whole),
            pl.BlockSpec((width // 2, 3 * LANES), whole),
            pl.BlockSpec((width // 2, 3 * LANES), whole),
        ]
        + [anywhere] * len(values),
        out_shape=[
            jax.ShapeDtypeStruct((rows, 3 * LANES), BF16),
            jax.ShapeDtypeStruct((1, 3 * LANES), F32),
            jax.ShapeDtypeStruct((width // 2, 3 * LANES), BF16),
            jax.ShapeDtypeStruct((width // 2, 3 * LANES), BF16),
        ]
        + [jax.ShapeDtypeStruct(v.shape, v.dtype) for v in values],
        scratch_shapes=[
            pltpu.VMEM((2, 2 * LANES, rows), BF16),
            pltpu.VMEM((2, 2 * LANES, rows), BF16),
            pltpu.VMEM((LANES, rows), F32),
            pltpu.VMEM((span // 2, LANES), BF16),
            pltpu.VMEM((span // 2, LANES), BF16),
            pltpu.VMEM((span // 2, 2 * LANES), BF16),
        ]
        + [pltpu.VMEM((span, 2 * LANES), BF16)] * 6
        + [pltpu.VMEM((size // 2, 2, width // size, 3 * LANES), BF16)]
        + [pltpu.VMEM(tokens.shape, BF16)]
        + [pltpu.SemaphoreType.DMA((2, len(values) + 6)), pltpu.SemaphoreType.DMA((1,))],
        compiler_params=pltpu.CompilerParams(
            vmem_limit_bytes=60 << 20,
            collective_id=collective_id,
            has_side_effects=True,
        ),
        cost_estimate=pl.CostEstimate(
            flops=28 * rows * keys * LANES,
            bytes_accessed=8 * keys * LANES + 12 * rows * LANES,
            transcendentals=2 * rows * keys,
        ),
        name="attend_back",
    )(queries, grads, context, lse, *blocks, *blocks, tokens, *values)


def tail_kernel(plans, widths, *refs):
    chains = len(plans)
    groups = len(widths)
    pieces = sum(len(part) for part in widths)
    last = groups - 1
    last_piece = widths[last][-1]
    wide = 3 * LANES

    def take(number):
        nonlocal refs
        taken, refs = refs[:number], refs[number:]
        return taken

    joined_refs, other_refs = take(groups), take(last)
    own_weights, other_weights, base_refs = take(pieces), take(pieces - 1), take(CHUNKS)
    keep_refs, cargo_refs = take(chains), take(chains)
    total_ref = take(1)[0]
    result_refs = take(chains)
    rows_refs, weight_refs, last_rows, last_weights = take(2), take(2), take(2), take(2)
    base_ref = take(1)[0]
    hops = [[take(3) for _ in plan] for plan in plans]
    semaphores, local = refs
    links = sorted({("dp", bit) for plan in plans for bit, _, _ in plan} | {("tensor", 0)})
    greet(links)
    last_copy = send(joined_refs[last], last_rows[1], semaphores, 0, "tensor", 0)
    last_copy.start()
    weight_copy = send(
        own_weights[pieces - 1],
        last_weights[1].at[:, wide - last_piece :],
        semaphores,
        1,
        "tensor",
        0,
    )
    weight_copy.start()
    count = 2
    flights = []
    for chain, plan in enumerate(plans):
        flights.append([])
        for level, (bit, _, _) in enumerate(plan):
            land, out, _ = hops[chain][level]
            source = cargo_refs[chain] if level == 0 else out
            flights[chain].append(send(source, land, semaphores, count, "dp", bit))
            count += 1
        flights[chain][0].start()
    loads = []

    def load(source, target):
        copy = pltpu.make_async_copy(source, target, local.at[len(loads)])
        copy.start()
        loads.append(copy)

    for group in range(last):
        cols = slice(group * wide, (group + 1) * wide)
        load(joined_refs[group], rows_refs[0].at[:, cols])
        load(other_refs[group], rows_refs[1].at[:, cols])
    for side, parts in enumerate((list(own_weights), list(other_weights))):
        for group in range(groups):
            target = last_weights[side] if group == last else weight_refs[side]
            base = 0 if group == last else group * wide
            for piece in widths[group]:
                if not parts:
                    continue
                load(parts.pop(0), target.at[:, base : base + piece])
                base += piece
    load(joined_refs[last], last_rows[0])
    for part in range(CHUNKS):
        height = base_refs[part].shape[0]
        load(base_refs[part], base_ref.at[part * height : (part + 1) * height, :])

    def advance(level):
        for chain, plan in enumerate(plans):
            if level >= len(plan):
                continue
            flights[chain][level].wait()
            land = hops[chain][level][0]
            keep = keep_refs[chain] if level == 0 else None
            if level == 0:
                held = keep[...].astype(F32)
            else:
                bit, high, low = plan[level]
                own = lax.axis_index("dp") // (1 << bit) % 2
                held = hops[chain][level][2][:, own].reshape(land.shape)
            whole = held + land[...].astype(F32)
            if level == len(plan) - 1:
                result_refs[chain][...] = whole
                continue
            bit, high, low = plan[level + 1]
            _, out, split = hops[chain][level + 1]
            own = lax.axis_index("dp") // (1 << bit) % 2
            split[...] = whole.reshape(split.shape)
            out[...] = split[:, 1 - own].reshape(out.shape).astype(out.dtype)
        for flight in flights:
            if level + 1 < len(flight):
                flight[level + 1].start()

    for copy in loads:
        copy.wait()
    tile = total_ref.shape[0] // 4

    def early(index, carry):
        band = pl.ds(pl.multiple_of(index * tile, tile), tile)
        total_ref[band, :] = dot(rows_refs[0][band, :], weight_refs[0][...], NT) + dot(
            rows_refs[1][band, :], weight_refs[1][...], NT
        )
        return carry

    def late(index, carry):
        band = pl.ds(pl.multiple_of(index * tile, tile), tile)
        last_part = dot(last_rows[0][band, :], last_weights[0][...], NT) + dot(
            last_rows[1][band, :], last_weights[1][...], NT
        )
        total_ref[band, :] = base_ref[band, :] + (total_ref[band, :] + last_part)
        return carry

    depth = max(len(plan) for plan in plans)
    lax.fori_loop(0, 2, early, 0)
    advance(0)
    lax.fori_loop(2, 4, early, 0)
    for level in range(1, depth - 1):
        advance(level)
    last_copy.wait()
    weight_copy.wait()
    lax.fori_loop(0, 4, late, 0)
    advance(depth - 1)


def tail(joined, others, own_weights, other_weights, base, chains, collective_id):
    groups = len(joined)
    rows, wide = joined[0].shape
    width = own_weights[0][0].shape[0]
    widths = [[piece.shape[1] for piece in part] for part in own_weights]
    own_weights = [piece for part in own_weights for piece in part]
    other_weights = [piece for part in other_weights for piece in part]
    size = lax.axis_size("dp")
    plans, scratch, results = [], [], []
    for chain in chains:
        left = list(chain.left)
        high_bits = sorted(left + [chain.cargo[1][1]], reverse=True)
        count, part, cols = chain.keep.shape[0], chain.part, chain.keep.shape[1]
        plan = []
        for bit in [chain.cargo[1][1]] + chain.order:
            high = 1 << high_bits.index(bit)
            high_bits.remove(bit)
            held = part << len(high_bits)
            low = held // high
            plan.append((bit, high, low))
            scratch += [
                pltpu.VMEM((held, cols), chain.wire),
                pltpu.VMEM((held, cols), chain.wire),
                pltpu.VMEM((high, 2, low, cols), F32),
            ]
        plans.append(plan)
        results.append(jax.ShapeDtypeStruct((part, cols), F32))
    anywhere = pl.BlockSpec(memory_space=pl.ANY)
    inside = pl.BlockSpec(memory_space=pltpu.VMEM)
    values = [*joined, *others, *own_weights, *other_weights, *base]
    loads = 2 * (groups - 1) + 2 * len(own_weights) + CHUNKS
    hops = sum(len(plan) for plan in plans)
    return pl.pallas_call(
        functools.partial(tail_kernel, plans, widths),
        in_specs=[anywhere] * len(values)
        + [inside] * len(chains)
        + [anywhere] * len(chains),
        out_specs=[inside] * (1 + len(chains)),
        out_shape=[jax.ShapeDtypeStruct((rows, width), F32)] + results,
        scratch_shapes=[pltpu.VMEM((rows, (groups - 1) * wide), BF16)] * 2
        + [pltpu.VMEM((width, (groups - 1) * wide), BF16)] * 2
        + [pltpu.VMEM((rows, wide), BF16)] * 2
        + [pltpu.VMEM((width, wide), BF16)] * 2
        + [pltpu.VMEM((rows, width), F32)]
        + scratch
        + [pltpu.SemaphoreType.DMA((2, hops + 2)), pltpu.SemaphoreType.DMA((loads,))],
        compiler_params=pltpu.CompilerParams(
            vmem_limit_bytes=60 << 20, collective_id=collective_id, has_side_effects=True
        ),
        cost_estimate=pl.CostEstimate(
            flops=12 * groups * rows * width * LANES,
            bytes_accessed=32 << 20,
            transcendentals=0,
        ),
        name="tail",
    )(*values, *[c.keep for c in chains], *[c.cargo[0] for c in chains])


def body(
    tokens,
    proj_weight,
    query_bias,
    value_bias,
    out_weight,
    out_bias,
    first_gain,
    first_shift,
    up_weight,
    up_bias,
    down_weight,
    down_bias,
    second_gain,
    second_shift,
    cotangent,
):
    rows, width = tokens.shape
    heads, head_size = query_bias.shape
    local = heads * head_size
    groups = local // LANES
    scale = 1.0 / math.sqrt(head_size)
    query_weight = proj_weight[:, 0, :]
    key_weight = proj_weight[:, 1, :]
    value_weight = proj_weight[:, 2, :]
    value_shift = value_bias.reshape(local)

    side = lax.axis_index("tensor")

    def in_order(own, other, dim):
        return jnp.where(
            side == 0,
            jnp.concatenate([own, other], axis=dim),
            jnp.concatenate([other, own], axis=dim),
        )

    own_blocks, blocks, weights = [], [], []
    for group in range(groups):
        cols = slice(group * LANES, (group + 1) * LANES)
        weight = jnp.concatenate([key_weight[:, cols], value_weight[:, cols]], axis=1)
        pieces = [query_weight[:, cols], weight]
        if group > 0:
            pieces[1:] = [key_weight[:, cols], value_weight[:, cols]]
        weights.append(pieces)
        shift = jnp.concatenate([jnp.zeros((LANES,), F32), value_shift[cols]])
        own_blocks.append((dot(tokens, weight, NN) + shift).astype(BF16))
    for own in own_blocks:
        across = flip(own, "dp", 1)
        blocks.append((own, flip(own, "dp", 0), across, flip(across, "dp", 0)))
    queries = (dot(tokens, query_weight, NN) + query_bias.reshape(local)).astype(BF16)
    out_other = flip(out_weight, "tensor", 0)
    out_whole = in_order(out_weight, out_other, 0)

    outs, own_context, other_context = [], [], []
    across = ("tensor", 0)
    ahead = jnp.concatenate([weights[1][2], *weights[3][:2]], axis=1)
    ahead = flip(ahead, "tensor", 0)
    for group in range(groups):
        if group > 0:
            queries = after(queries, outs[-1][1])
        if group == groups - 2:
            queries = after(queries, out_other)
        if group == groups - 1:
            queries = after(queries, ahead)
        out, lse = attend(queries, group, blocks[group], scale)
        outs.append((out, lse))
        own_context.append(out.astype(BF16))
        other_context.append(flip(own_context[-1], "tensor", 0))
    context = jnp.concatenate(own_context, axis=1)
    context_whole = in_order(context, jnp.concatenate(other_context, axis=1), 1)

    step = rows // CHUNKS
    cuts = [slice(i * step, (i + 1) * step) for i in range(CHUNKS)]
    firsts, lows, actives, active_lows, feed_lows, feed_others = [], [], [], [], [], []
    done = context_whole
    for cut in cuts:
        attention = dot(after(context_whole[cut], done), out_whole, NN) + out_bias
        first = jax.vjp(
            layer_norm, tokens[cut].astype(F32) + attention, first_gain, first_shift
        )
        low = first[0].astype(BF16)
        hidden = dot(low, up_weight, NN) + up_bias.reshape(-1)
        active = jax.vjp(gelu_tanh, hidden)
        active_low = active[0].astype(BF16)
        feed_low = dot(active_low, down_weight, NN).astype(BF16)
        done = feed_low
        firsts.append(first)
        lows.append(low)
        actives.append(active)
        active_lows.append(active_low)
        feed_lows.append(feed_low)
        feed_others.append(flip(feed_low, "tensor", 0))
    seconds, second_grads, feed_grads, hidden_lows, grad_lows, grad_others = (
        [], [], [], [], [], [],
    )
    for i, cut in enumerate(cuts):
        other = after(feed_others[i], done)
        feed = feed_lows[i].astype(F32) + other.astype(F32) + down_bias
        second, second_back = jax.vjp(
            layer_norm, firsts[i][0] + feed, second_gain, second_shift
        )
        grads = second_back(cotangent[cut].astype(F32))
        feed_grad = grads[0].astype(BF16)
        hidden_low = actives[i][1](dot(feed_grad, down_weight, NT))[0].astype(BF16)
        grad_low = dot(hidden_low, up_weight, NT).astype(BF16)
        done = grad_low
        seconds.append(second.astype(BF16))
        second_grads.append(grads)
        feed_grads.append(feed_grad)
        hidden_lows.append(hidden_low)
        grad_lows.append(grad_low)
        grad_others.append(flip(grad_low, "tensor", 0))
    layer_output = jnp.concatenate(seconds, axis=0)
    feed_grad = after(jnp.concatenate(feed_grads, axis=0), done)
    active_low = jnp.concatenate(active_lows, axis=0)
    down_rows = dot(feed_grad, active_low, TN).astype(BF16)
    down_scatter = Scatter(down_rows, BF16)
    down_flight = down_scatter.fly()
    hidden_low = after(jnp.concatenate(hidden_lows, axis=0), down_rows)
    first_low = jnp.concatenate(lows, axis=0)
    up_rows = dot(first_low, hidden_low, TN).astype(BF16)
    up_scatter = Scatter(up_rows, BF16, True)
    up_flight = up_scatter.fly()
    downbias_grad = jnp.sum(feed_grad.astype(F32), axis=0)
    upbias_grad = jnp.sum(hidden_low.astype(F32), axis=0)
    secondgain_grad = sum(grads[1] for grads in second_grads)
    secondshift_grad = sum(grads[2] for grads in second_grads)
    done = down_scatter.gather(after(down_flight, up_rows))
    middle = down_rows.shape[1] // 2
    down_parts = [
        Columns(down_scatter, slice(None, middle)),
        Columns(down_scatter, slice(middle, None), True),
    ]

    attention_backs, firstgain_parts, firstshift_parts = [], [], []
    for i in range(CHUNKS):
        other = after(grad_others[i], done)
        grad = second_grads[i][0] + (grad_lows[i].astype(F32) + other.astype(F32))
        grads = firsts[i][1](grad)
        attention_backs.append(grads[0])
        firstgain_parts.append(grads[1])
        firstshift_parts.append(grads[2])
    attention_back = jnp.concatenate(attention_backs, axis=0)
    firstgain_grad = sum(firstgain_parts)
    firstshift_grad = sum(firstshift_parts)
    attention_grad = attention_back.astype(BF16)
    outbias_grad = jnp.sum(attention_grad.astype(F32), axis=0)
    context_grad = dot(attention_grad, out_weight, NT).astype(BF16)
    out_rows = dot(attention_grad, context, TN).astype(BF16)
    out_scatter = Scatter(out_rows, BF16)
    up_scatter.land(after(up_flight, out_rows))

    size = lax.axis_size("dp")

    def by_dp(vector, leading):
        return (
            vector.reshape(leading, size, -1).transpose(1, 0, 2).reshape(size, -1)
        )

    def unpack(packed, pieces):
        vectors, at = [], 0
        for part, leading in pieces:
            piece = packed[at : at + part.shape[1]]
            at += part.shape[1]
            vectors.append(piece.reshape(leading, -1) if leading else piece)
        return vectors

    units = up_bias.shape[0]
    early = [
        (by_dp(outbias_grad, 1), 0),
        (by_dp(firstgain_grad, 1), 0),
        (by_dp(firstshift_grad, 1), 0),
        (by_dp(upbias_grad, units), units),
        (by_dp(downbias_grad, 1), 0),
        (by_dp(secondgain_grad, 1), 0),
        (by_dp(secondshift_grad, 1), 0),
    ]
    early_scatter = Scatter(jnp.concatenate([part for part, _ in early], axis=1), F32)

    tokens_turned = tokens.T
    trips = [[(0, 0), (0, 1), (2, 0), (1, 1)], [(1, 0)], [(2, 1)], [(2, 2)]]
    ahead = [ahead[:, i * LANES : (i + 1) * LANES] for i in range(3)]
    other_weights = [[None] * 2, [None, None, ahead[0]], [None] * 3, ahead[1:]]
    joined, others, sums, proj_scatters = [], [], [], []
    active = [up_scatter, out_scatter, early_scatter, down_parts[0]]
    for group in range(groups):
        cargo = [scatter.cargo for scatter in active]
        cargo += [(weights[place][piece], across) for place, piece in trips[group]]
        if group > 0:
            cargo.append((joined[-1], across))
        out, lse = outs[group]
        rows_back, row_sums, keep, outgoing, *arrived = attend_back(
            queries,
            context_grad,
            tokens_turned,
            group,
            out,
            lse,
            blocks[group],
            scale,
            cargo,
            group,
        )
        for scatter in active:
            scatter.land(arrived.pop(0))
        for place, piece in trips[group]:
            other_weights[place][piece] = arrived.pop(0)
        if group > 0:
            others.append(arrived.pop(0))
        joined.append(rows_back)
        sums.append(row_sums.reshape(3, LANES))
        proj_scatters.append(Ready(keep, outgoing, group < groups - 1))
        active.append(proj_scatters[-1])
        if group == 1:
            active.append(down_parts[1])
        active = [scatter for scatter in active if scatter.cargo is not None]
    sums = jnp.stack(sums, axis=1).reshape(3, local)
    late = [(by_dp(sums[0], heads), heads), (by_dp(sums[2], heads), heads)]
    late_rows = jnp.concatenate([part for part, _ in late], axis=1)
    late_rows = jnp.pad(late_rows[:, None, :], ((0, 0), (0, 7), (0, 0)))
    late_scatter = Scatter(late_rows.reshape(8 * size, -1), F32)
    active.append(late_scatter)

    tokens_grad, *ends = tail(
        joined, others, weights, other_weights, attention_backs, active, groups
    )
    for scatter, value in zip(active, ends):
        scatter.whole = value
    outweight_grad = out_scatter.result()
    upweight_grad = up_scatter.result()
    downweight_grad = jnp.concatenate([part.result() for part in down_parts], axis=1)
    proj_grad = jnp.stack(
        [scatter.result().reshape(-1, 3, LANES) for scatter in proj_scatters], axis=2
    )
    vectors = unpack(late_scatter.result()[0], late) + unpack(
        early_scatter.result()[0], early
    )
    return (
        layer_output,
        tokens_grad,
        proj_grad.reshape(width // size, 3, local),
        vectors[0],
        vectors[1],
        outweight_grad.T,
        vectors[2],
        vectors[3],
        vectors[4],
        upweight_grad,
        vectors[5],
        downweight_grad.T,
        vectors[6],
        vectors[7],
        vectors[8],
    )


def solution(mesh):
    return jax.shard_map(
        body,
        mesh=mesh,
        in_specs=(
            P("dp", None),
            P(None, None, "tensor"),
            P("tensor", None),
            P("tensor", None),
            P("tensor", None),
            P(),
            P(),
            P(),
            P(None, "tensor"),
            P("tensor", None),
            P("tensor", None),
            P(),
            P(),
            P(),
            P("dp", None),
        ),
        out_specs=(
            P("dp", None),
            P("dp", None),
            P("dp", None, "tensor"),
            P("tensor", "dp"),
            P("tensor", "dp"),
            P("tensor", "dp"),
            P("dp"),
            P("dp"),
            P("dp"),
            P("dp", "tensor"),
            P("tensor", "dp"),
            P("tensor", "dp"),
            P("dp"),
            P("dp"),
            P("dp"),
        ),
        check_vma=False,
    )
```

```python
import functools
import math

import jax
import jax.numpy as jnp
from jax import lax
from jax.experimental import pallas as pl
from jax.experimental.pallas import tpu as pltpu
from jax.sharding import PartitionSpec as P

EPS = 1e-12
F32 = jnp.float32
BF16 = jnp.bfloat16
LANES = 128
HALF = 64
SOURCES = 4
CHUNKS = 3
NN = (((1,), (0,)), ((), ()))
NT = (((1,), (1,)), ((), ()))
TN = (((0,), (0,)), ((), ()))
MESH = pl.DeviceIdType.MESH


def dot(left, right, dims):
    return lax.dot_general(left, right, dims, preferred_element_type=F32)


def flip(value, axis, bit):
    pairs = [(source, source ^ (1 << bit)) for source in range(lax.axis_size(axis))]
    return lax.ppermute(value, axis, pairs)


def pair_sum(partial):
    low = partial.astype(BF16)
    return low.astype(F32) + flip(low, "tensor", 0).astype(F32)


def partner(axis, bit):
    place = lax.axis_index(axis)
    return {axis: place + (1 - 2 * (place // (1 << bit) % 2)) * (1 << bit)}


def greet(links):
    barrier = pltpu.get_barrier_semaphore()
    for axis, bit in links:
        pl.semaphore_signal(
            barrier, inc=1, device_id=partner(axis, bit), device_id_type=MESH
        )
    pl.semaphore_wait(barrier, len(links))


def send(source, target, semaphores, index, axis, bit):
    return pltpu.make_async_remote_copy(
        src_ref=source,
        dst_ref=target,
        send_sem=semaphores.at[0, index],
        recv_sem=semaphores.at[1, index],
        device_id=partner(axis, bit),
        device_id_type=MESH,
    )


def after(value, *earlier):
    return lax.optimization_barrier((value, earlier))[0]


def sides(value, bit, left):
    view = value.reshape(1 << left.index(bit), 2, -1, value.shape[-1])
    own = lax.axis_index("dp") >> bit & 1
    return [
        lax.dynamic_index_in_dim(view, side, 1, keepdims=False).reshape(
            -1, view.shape[-1]
        )
        for side in (own, 1 - own)
    ]


class Scatter:
    def __init__(self, rows, wire, far_first=False):
        size = lax.axis_size("dp")
        bits = size.bit_length() - 1
        self.part = rows.shape[0] // size
        self.whole = rows
        self.wire = wire
        self.left = list(range(bits))[::-1]
        self.order = list(range(bits))
        if far_first and bits > 2:
            self.order = [0] + self.order[2:] + [1]
        self.split()

    def split(self, ready=None):
        self.cargo = None
        if not self.order:
            return
        bit = self.order.pop(0)
        if ready is None:
            ready = sides(self.whole, bit, self.left)
        self.left.remove(bit)
        self.keep = ready[0]
        self.cargo = (ready[1].astype(self.wire), ("dp", bit))

    def gather(self, arrived):
        self.whole = self.keep.astype(F32) + arrived.astype(F32)
        return self.whole

    def land(self, arrived):
        if not self.order:
            self.cargo = None
            return self.gather(arrived)
        bit = self.order[0]
        kept, sent = sides(self.keep, bit, self.left), sides(arrived, bit, self.left)
        self.split([a.astype(F32) + b.astype(F32) for a, b in zip(kept, sent)])

    def fly(self):
        value, (axis, bit) = self.cargo
        return flip(value, axis, bit)

    def result(self):
        return self.whole


class Columns(Scatter):
    def __init__(self, other, cols, far_first=False):
        self.part, self.wire = other.part, other.wire
        self.left, self.order = list(other.left), list(other.order)
        if far_first and len(self.order) > 1:
            self.order = self.order[1:] + self.order[:1]
        self.whole = other.whole[:, cols]
        self.split()


class Ready(Scatter):
    def __init__(self, keep, out, far_first):
        size = lax.axis_size("dp")
        bits = size.bit_length() - 1
        self.part = 2 * keep.shape[0] // size
        self.wire = out.dtype
        self.left = list(range(bits))[::-1]
        self.order = list(range(bits))
        if far_first and bits > 2:
            self.order = [0] + self.order[2:] + [1]
        self.split([keep, out])


def layer_norm(rows, gain, shift):
    mean = jnp.mean(rows, axis=-1, keepdims=True)
    centered = rows - mean
    spread = jnp.mean(centered * centered, axis=-1, keepdims=True)
    return centered * lax.rsqrt(spread + EPS) * gain + shift


def gelu_tanh(values):
    return jax.nn.gelu(values, approximate=True)


def column_sums(values):
    return dot(jnp.ones((16, values.shape[0]), BF16), values, NN)[0]


def head_lanes(shape, head):
    lane = lax.broadcasted_iota(jnp.int32, shape, 1)
    return (lane < HALF) if head == 0 else (lane >= HALF)


def forward_kernel(scale, tile, *refs):
    q_ref = refs[0]
    k_refs = refs[1 : 1 + SOURCES]
    v_refs = refs[1 + SOURCES : 1 + 2 * SOURCES]
    o_ref, lse_ref, s_ref, vt_ref = refs[1 + 2 * SOURCES :]
    span = k_refs[0].shape[0]

    @pl.when(pl.program_id(0) == 0)
    def _():
        for source in range(SOURCES):
            vt_ref[:LANES, source * span : (source + 1) * span] = jnp.transpose(
                v_refs[source][...]
            )
        vt_ref[LANES:, :] = jnp.ones((vt_ref.shape[0] - LANES, vt_ref.shape[1]), BF16)

    q = q_ref[...] * scale
    outs = []
    for head in range(2):
        own = head_lanes(q.shape, head)
        qt = jnp.transpose(jnp.where(own, q, jnp.zeros_like(q)))
        peak = None
        for source in range(SOURCES):
            for start in range(0, span, tile):
                scores = dot(k_refs[source][start : start + tile, :], qt, NN)
                base = source * span + start
                s_ref[head, base : base + tile, :] = scores
                top = jnp.max(scores, axis=0, keepdims=True)
                peak = top if peak is None else jnp.maximum(peak, top)
        total = None
        for start in range(0, SOURCES * span, tile):
            weights = jnp.exp(s_ref[head, start : start + tile, :] - peak).astype(BF16)
            part = dot(vt_ref[:, start : start + tile], weights, NN)
            total = part if total is None else total + part
        mass = total[LANES : LANES + 1, :]
        outs.append(total[head * HALF : (head + 1) * HALF, :] / mass)
        lse_ref[head, :] = (peak + jnp.log(mass))[0]
    o_ref[...] = jnp.transpose(jnp.concatenate(outs, 0))


def attend(queries, group, blocks, scale):
    rows = queries.shape[0]
    span = blocks[0].shape[0]
    tq = rows // 2
    keys = SOURCES * span
    return pl.pallas_call(
        functools.partial(forward_kernel, scale, span // 2),
        grid=(rows // tq,),
        in_specs=[pl.BlockSpec((tq, LANES), lambda i: (i, group))]
        + [pl.BlockSpec((span, LANES), lambda i: (0, 0))] * SOURCES
        + [pl.BlockSpec((span, LANES), lambda i: (0, 1))] * SOURCES,
        out_specs=[
            pl.BlockSpec((tq, LANES), lambda i: (i, 0)),
            pl.BlockSpec((2, tq), lambda i: (0, i)),
        ],
        out_shape=[
            jax.ShapeDtypeStruct((rows, LANES), F32),
            jax.ShapeDtypeStruct((2, rows), F32),
        ],
        scratch_shapes=[
            pltpu.VMEM((2, keys, tq), F32),
            pltpu.VMEM((LANES + 16, keys), BF16),
        ],
        compiler_params=pltpu.CompilerParams(vmem_limit_bytes=40 << 20),
        cost_estimate=pl.CostEstimate(
            flops=16 * rows * keys * LANES,
            bytes_accessed=4 * (keys + rows) * LANES + 4 * rows * LANES,
            transcendentals=2 * rows * keys,
        ),
        name="attend",
    )(queries, *blocks, *blocks)


def thirds(value):
    high = value.astype(BF16).astype(F32)
    rest = value - high
    middle = rest.astype(BF16).astype(F32)
    return high, middle, rest - middle


def backward_kernel(scale, tile, links, *refs):
    count = len(links)
    q_ref, g_ref, o_ref, lse_ref = refs[:4]
    k_refs = refs[4 : 4 + SOURCES]
    v_refs = refs[4 + SOURCES : 4 + 2 * SOURCES]
    tokens_ref = refs[4 + 2 * SOURCES]
    refs = refs[5 + 2 * SOURCES :]
    cargo_refs, refs = refs[:count], refs[count:]
    joined_ref, sums_ref, keep_ref, out_ref = refs[:4]
    landing_refs, refs = refs[4 : 4 + count], refs[4 + count :]
    qt_ref, gt_ref, dqt_ref, k_ref, v_ref, d_ref = refs[:6]
    diagonal_ref, cross_ref, beside_ref = refs[6:9]
    diagonal_in, cross_in, beside_in, product_ref, turned_ref, semaphores, local = refs[9:]
    turned_copy = pltpu.make_async_copy(tokens_ref, turned_ref, local.at[0])
    step = pl.program_id(0)
    rows = q_ref.shape[0]
    own_links = [("dp", 0), ("dp", 1)]
    copies = [
        send(cargo_refs[i], landing_refs[i], semaphores, i, *links[i])
        for i in range(count)
    ]
    halves = [slice(half * tile, (half + 1) * tile) for half in range(2)]

    def part_copies(source, target, first, bit):
        return [
            send(source.at[rows], target.at[rows], semaphores, count + first + i, "dp", bit)
            for i, rows in enumerate(halves)
        ]

    diagonal_copies = part_copies(diagonal_ref, diagonal_in, 0, 0)
    cross_copies = part_copies(cross_ref, cross_in, 2, 1)
    beside_copies = part_copies(beside_ref, beside_in, 4, 0)

    @pl.when(step == 0)
    def _():
        greet(sorted(set(own_links + links)))
        for copy in copies:
            copy.start()
        turned_copy.start()
        q = q_ref[...] * scale
        g = g_ref[...]
        products = jnp.transpose(g.astype(F32) * o_ref[...])
        row = lax.broadcasted_iota(jnp.int32, (LANES, rows), 0)
        for head in range(2):
            own = head_lanes(q.shape, head)
            qt_ref[head, :LANES, :] = jnp.transpose(jnp.where(own, q, jnp.zeros_like(q)))
            gt_ref[head, :LANES, :] = jnp.transpose(jnp.where(own, g, jnp.zeros_like(g)))
            centre = jnp.sum(
                products[head * HALF : (head + 1) * HALF], axis=0, keepdims=True
            )
            for ref, value in (
                (qt_ref, -lse_ref[head : head + 1, :]),
                (gt_ref, -centre),
            ):
                high, middle, low = thirds(value)
                ref[head, LANES:, :] = jnp.where(
                    row == 0,
                    high,
                    jnp.where(row == 1, middle, jnp.where(row == 2, low, 0.0)),
                ).astype(BF16)
        dqt_ref[...] = jnp.zeros_like(dqt_ref)

    for first, later in ((1, diagonal_copies), (3, cross_copies), (5, beside_copies)):
        for half in range(2):

            @pl.when(step == first + half)
            def _():
                later[half].start()

    for source in range(SOURCES):
        for half in range(2):

            @pl.when(step == 2 * (SOURCES - 1 - source) + half)
            def _():
                k_ref[...] = k_refs[source][halves[half], :]
                v_ref[...] = v_refs[source][halves[half], :]

    k = k_ref[...]
    v = v_ref[...]
    one = jnp.ones_like(k)
    k_wide = jnp.concatenate([k, one], 1)
    v_wide = jnp.concatenate([v, one], 1)
    kt = jnp.transpose(k)
    parts = []
    for head in range(2):
        probs = jnp.exp(dot(k_wide, qt_ref[head], NN))
        centred = dot(v_wide, gt_ref[head], NN)
        score_grad = (probs * centred).astype(BF16)
        parts.append(
            (
                dot(score_grad, q_ref[...], NN),
                dot(probs.astype(BF16), g_ref[...], NN),
            )
        )
        dqt_ref[head * HALF : (head + 1) * HALF, :] += dot(
            kt[head * HALF : (head + 1) * HALF, :], score_grad, NN
        )
    first = head_lanes(k.shape, 0)
    d_ref[:, :LANES] = (jnp.where(first, parts[0][0], parts[1][0]) * scale).astype(BF16)
    d_ref[:, LANES:] = jnp.where(first, parts[0][1], parts[1][1]).astype(BF16)

    for half in range(2):
        band = halves[half]

        @pl.when(step == half)
        def _():
            diagonal_ref[band, :] = d_ref[...]

        @pl.when(step == 2 + half)
        def _():
            diagonal_copies[half].wait()
            cross_ref[band, :] = (
                d_ref[...].astype(F32) + diagonal_in[band, :].astype(F32)
            ).astype(BF16)

        @pl.when(step == 4 + half)
        def _():
            beside_ref[band, :] = d_ref[...]

        @pl.when(step == 6 + half)
        def _():
            beside_copies[half].wait()
            cross_copies[half].wait()
            joined_ref[band, LANES:] = (
                d_ref[...].astype(F32)
                + beside_in[band, :].astype(F32)
                + cross_in[band, :].astype(F32)
            ).astype(BF16)

    @pl.when(step == 7)
    def _():
        joined_ref[:, :LANES] = (jnp.transpose(dqt_ref[...]) * scale).astype(BF16)
        joined = joined_ref[...]
        sums_ref[...] = jnp.sum(joined.astype(F32), axis=0, keepdims=True)
        turned_copy.wait()
        pairs, _, part, _ = product_ref.shape
        for pair in range(0, pairs, 2):
            band = turned_ref[2 * pair * part : 2 * (pair + 2) * part, :]
            product_ref[pair : pair + 2] = (
                dot(band, joined, NN).astype(BF16).reshape(2, 2, part, 3 * LANES)
            )
        side = lax.axis_index("dp") % 2
        keep_ref[...] = product_ref[:, side].reshape(keep_ref.shape)
        out_ref[...] = product_ref[:, 1 - side].reshape(out_ref.shape)
        for copy in copies:
            copy.wait()


def attend_back(
    queries, grads, tokens, group, context, lse, blocks, scale, cargo, collective_id
):
    rows = queries.shape[0]
    span = blocks[0].shape[0]
    keys = SOURCES * span
    size, width = lax.axis_size("dp"), tokens.shape[0]
    whole = lambda i: (0, 0)
    links = [link for _, link in cargo]
    values = [value for value, _ in cargo]
    anywhere = pl.BlockSpec(memory_space=pl.ANY)
    return pl.pallas_call(
        functools.partial(backward_kernel, scale, span // 2, links),
        grid=(2 * SOURCES,),
        in_specs=[
            pl.BlockSpec((rows, LANES), lambda i: (0, group)),
            pl.BlockSpec((rows, LANES), lambda i: (0, group)),
            pl.BlockSpec((rows, LANES), whole),
            pl.BlockSpec((2, rows), whole),
        ]
        + [pl.BlockSpec((span, LANES), whole)] * SOURCES
        + [pl.BlockSpec((span, LANES), lambda i: (0, 1))] * SOURCES
        + [anywhere] * (1 + len(values)),
        out_specs=[
            pl.BlockSpec((rows, 3 * LANES), whole),
            pl.BlockSpec((1, 3 * LANES), whole),
            pl.BlockSpec((width // 2, 3 * LANES), whole),
            pl.BlockSpec((width // 2, 3 * LANES), whole),
        ]
        + [anywhere] * len(values),
        out_shape=[
            jax.ShapeDtypeStruct((rows, 3 * LANES), BF16),
            jax.ShapeDtypeStruct((1, 3 * LANES), F32),
            jax.ShapeDtypeStruct((width // 2, 3 * LANES), BF16),
            jax.ShapeDtypeStruct((width // 2, 3 * LANES), BF16),
        ]
        + [jax.ShapeDtypeStruct(v.shape, v.dtype) for v in values],
        scratch_shapes=[
            pltpu.VMEM((2, 2 * LANES, rows), BF16),
            pltpu.VMEM((2, 2 * LANES, rows), BF16),
            pltpu.VMEM((LANES, rows), F32),
            pltpu.VMEM((span // 2, LANES), BF16),
            pltpu.VMEM((span // 2, LANES), BF16),
            pltpu.VMEM((span // 2, 2 * LANES), BF16),
        ]
        + [pltpu.VMEM((span, 2 * LANES), BF16)] * 6
        + [pltpu.VMEM((size // 2, 2, width // size, 3 * LANES), BF16)]
        + [pltpu.VMEM(tokens.shape, BF16)]
        + [pltpu.SemaphoreType.DMA((2, len(values) + 6)), pltpu.SemaphoreType.DMA((1,))],
        compiler_params=pltpu.CompilerParams(
            vmem_limit_bytes=60 << 20,
            collective_id=collective_id,
            has_side_effects=True,
        ),
        cost_estimate=pl.CostEstimate(
            flops=28 * rows * keys * LANES,
            bytes_accessed=8 * keys * LANES + 12 * rows * LANES,
            transcendentals=2 * rows * keys,
        ),
        name="attend_back",
    )(queries, grads, context, lse, *blocks, *blocks, tokens, *values)


def tail_kernel(plans, widths, merged, *refs):
    chains = len(plans)
    groups = len(widths)
    pieces = sum(len(part) for part in widths)
    last = groups - 1
    last_piece = widths[last][-1]
    wide = 3 * LANES

    def take(number):
        nonlocal refs
        taken, refs = refs[:number], refs[number:]
        return taken

    joined_refs, other_refs = take(groups), take(last)
    own_weights, other_weights, base_refs = take(pieces), take(pieces - 1), take(CHUNKS)
    keep_refs, cargo_refs = take(chains), take(chains)
    total_ref = take(1)[0]
    merged_ref = take(1)[0]
    result_refs = list(take(chains - len(merged)))
    result_refs = [
        None if chain in merged else result_refs.pop(0) for chain in range(chains)
    ]
    rows_refs, weight_refs, last_rows, last_weights = take(2), take(2), take(2), take(2)
    base_ref = take(1)[0]
    hops = [[take(3) for _ in plan] for plan in plans]
    semaphores, local = refs
    links = sorted({("dp", bit) for plan in plans for bit, _, _ in plan} | {("tensor", 0)})
    greet(links)
    last_copy = send(joined_refs[last], last_rows[1], semaphores, 0, "tensor", 0)
    last_copy.start()
    weight_copy = send(
        own_weights[pieces - 1],
        last_weights[1].at[:, wide - last_piece :],
        semaphores,
        1,
        "tensor",
        0,
    )
    weight_copy.start()
    count = 2
    flights = []
    for chain, plan in enumerate(plans):
        flights.append([])
        for level, (bit, _, _) in enumerate(plan):
            land, out, _ = hops[chain][level]
            source = cargo_refs[chain] if level == 0 else out
            flights[chain].append(send(source, land, semaphores, count, "dp", bit))
            count += 1
        flights[chain][0].start()
    loads = []

    def load(source, target):
        copy = pltpu.make_async_copy(source, target, local.at[len(loads)])
        copy.start()
        loads.append(copy)

    for group in range(last):
        cols = slice(group * wide, (group + 1) * wide)
        load(joined_refs[group], rows_refs[0].at[:, cols])
        load(other_refs[group], rows_refs[1].at[:, cols])
    for side, parts in enumerate((list(own_weights), list(other_weights))):
        for group in range(groups):
            target = last_weights[side] if group == last else weight_refs[side]
            base = 0 if group == last else group * wide
            for piece in widths[group]:
                if not parts:
                    continue
                load(parts.pop(0), target.at[:, base : base + piece])
                base += piece
    load(joined_refs[last], last_rows[0])
    top = 0
    for part in range(CHUNKS):
        height = base_refs[part].shape[0]
        load(base_refs[part], base_ref.at[top : top + height, :])
        top += height

    def advance(level):
        for chain, plan in enumerate(plans):
            if level >= len(plan):
                continue
            flights[chain][level].wait()
            land = hops[chain][level][0]
            keep = keep_refs[chain] if level == 0 else None
            if level == 0:
                held = keep[...].astype(F32)
            else:
                bit, high, low = plan[level]
                own = lax.axis_index("dp") // (1 << bit) % 2
                held = hops[chain][level][2][:, own].reshape(land.shape)
            whole = held + land[...].astype(F32)
            if level == len(plan) - 1:
                if chain not in merged:
                    result_refs[chain][...] = whole
                    continue
                for piece in range(3):
                    at = (piece * groups + merged.index(chain)) * LANES
                    merged_ref[:, at : at + LANES] = whole[
                        :, piece * LANES : (piece + 1) * LANES
                    ]
                continue
            bit, high, low = plan[level + 1]
            _, out, split = hops[chain][level + 1]
            own = lax.axis_index("dp") // (1 << bit) % 2
            split[...] = whole.reshape(split.shape)
            out[...] = split[:, 1 - own].reshape(out.shape).astype(out.dtype)
        for flight in flights:
            if level + 1 < len(flight):
                flight[level + 1].start()

    for copy in loads:
        copy.wait()
    tile = total_ref.shape[0] // 4

    def early(index, carry):
        band = pl.ds(pl.multiple_of(index * tile, tile), tile)
        total_ref[band, :] = dot(rows_refs[0][band, :], weight_refs[0][...], NT) + dot(
            rows_refs[1][band, :], weight_refs[1][...], NT
        )
        return carry

    def late(index, carry):
        band = pl.ds(pl.multiple_of(index * tile, tile), tile)
        last_part = dot(last_rows[0][band, :], last_weights[0][...], NT) + dot(
            last_rows[1][band, :], last_weights[1][...], NT
        )
        total_ref[band, :] = base_ref[band, :] + (total_ref[band, :] + last_part)
        return carry

    depth = max(len(plan) for plan in plans)
    lax.fori_loop(0, 2, early, 0)
    advance(0)
    lax.fori_loop(2, 4, early, 0)
    for level in range(1, depth - 1):
        advance(level)
    last_copy.wait()
    weight_copy.wait()
    lax.fori_loop(0, 4, late, 0)
    advance(depth - 1)


def tail(
    joined, others, own_weights, other_weights, base, chains, merged, collective_id
):
    groups = len(joined)
    rows, wide = joined[0].shape
    width = own_weights[0][0].shape[0]
    widths = [[piece.shape[1] for piece in part] for part in own_weights]
    own_weights = [piece for part in own_weights for piece in part]
    other_weights = [piece for part in other_weights for piece in part]
    size = lax.axis_size("dp")
    plans, scratch, results = [], [], []
    for chain in chains:
        left = list(chain.left)
        high_bits = sorted(left + [chain.cargo[1][1]], reverse=True)
        count, part, cols = chain.keep.shape[0], chain.part, chain.keep.shape[1]
        plan = []
        for bit in [chain.cargo[1][1]] + chain.order:
            high = 1 << high_bits.index(bit)
            high_bits.remove(bit)
            held = part << len(high_bits)
            low = held // high
            plan.append((bit, high, low))
            scratch += [
                pltpu.VMEM((held, cols), chain.wire),
                pltpu.VMEM((held, cols), chain.wire),
                pltpu.VMEM((high, 2, low, cols), F32),
            ]
        plans.append(plan)
        if chain not in merged:
            results.append(jax.ShapeDtypeStruct((part, cols), F32))
    results.insert(0, jax.ShapeDtypeStruct((merged[0].part, groups * wide), F32))
    anywhere = pl.BlockSpec(memory_space=pl.ANY)
    inside = pl.BlockSpec(memory_space=pltpu.VMEM)
    values = [*joined, *others, *own_weights, *other_weights, *base]
    loads = 2 * (groups - 1) + 2 * len(own_weights) + CHUNKS
    hops = sum(len(plan) for plan in plans)
    return pl.pallas_call(
        functools.partial(
            tail_kernel, plans, widths, [chains.index(chain) for chain in merged]
        ),
        in_specs=[anywhere] * len(values)
        + [inside] * len(chains)
        + [anywhere] * len(chains),
        out_specs=[inside] * (1 + len(results)),
        out_shape=[jax.ShapeDtypeStruct((rows, width), F32)] + results,
        scratch_shapes=[pltpu.VMEM((rows, (groups - 1) * wide), BF16)] * 2
        + [pltpu.VMEM((width, (groups - 1) * wide), BF16)] * 2
        + [pltpu.VMEM((rows, wide), BF16)] * 2
        + [pltpu.VMEM((width, wide), BF16)] * 2
        + [pltpu.VMEM((rows, width), F32)]
        + scratch
        + [pltpu.SemaphoreType.DMA((2, hops + 2)), pltpu.SemaphoreType.DMA((loads,))],
        compiler_params=pltpu.CompilerParams(
            vmem_limit_bytes=60 << 20, collective_id=collective_id, has_side_effects=True
        ),
        cost_estimate=pl.CostEstimate(
            flops=12 * groups * rows * width * LANES,
            bytes_accessed=32 << 20,
            transcendentals=0,
        ),
        name="tail",
    )(*values, *[c.keep for c in chains], *[c.cargo[0] for c in chains])


def body(
    tokens,
    proj_weight,
    query_bias,
    value_bias,
    out_weight,
    out_bias,
    first_gain,
    first_shift,
    up_weight,
    up_bias,
    down_weight,
    down_bias,
    second_gain,
    second_shift,
    cotangent,
):
    rows, width = tokens.shape
    heads, head_size = query_bias.shape
    local = heads * head_size
    groups = local // LANES
    scale = 1.0 / math.sqrt(head_size)
    query_weight = proj_weight[:, 0, :]
    key_weight = proj_weight[:, 1, :]
    value_weight = proj_weight[:, 2, :]
    value_shift = value_bias.reshape(local)

    side = lax.axis_index("tensor")

    def in_order(own, other, dim):
        return jnp.where(
            side == 0,
            jnp.concatenate([own, other], axis=dim),
            jnp.concatenate([other, own], axis=dim),
        )

    own_blocks, blocks, weights = [], [], []
    for group in range(groups):
        cols = slice(group * LANES, (group + 1) * LANES)
        weight = jnp.concatenate([key_weight[:, cols], value_weight[:, cols]], axis=1)
        pieces = [query_weight[:, cols], weight]
        if group > 0:
            pieces[1:] = [key_weight[:, cols], value_weight[:, cols]]
        weights.append(pieces)
        shift = jnp.concatenate([jnp.zeros((LANES,), F32), value_shift[cols]])
        own_blocks.append((dot(tokens, weight, NN) + shift).astype(BF16))
    for own in own_blocks:
        across = flip(own, "dp", 1)
        blocks.append((own, flip(own, "dp", 0), across, flip(across, "dp", 0)))
    queries = (dot(tokens, query_weight, NN) + query_bias.reshape(local)).astype(BF16)
    out_other = flip(out_weight, "tensor", 0)
    out_whole = in_order(out_weight, out_other, 0)

    outs, own_context, other_context = [], [], []
    across = ("tensor", 0)
    ahead = jnp.concatenate([weights[1][2], *weights[3][:2]], axis=1)
    ahead = flip(ahead, "tensor", 0)
    for group in range(groups):
        if group > 0:
            queries = after(queries, outs[-1][1])
        if group == groups - 2:
            queries = after(queries, out_other)
        if group == groups - 1:
            queries = after(queries, ahead)
        out, lse = attend(queries, group, blocks[group], scale)
        outs.append((out, lse))
        own_context.append(out.astype(BF16))
        other_context.append(flip(own_context[-1], "tensor", 0))
    context = jnp.concatenate(own_context, axis=1)
    context_whole = in_order(context, jnp.concatenate(other_context, axis=1), 1)

    edges = [0, rows // 4, 3 * rows // 4, rows]
    cuts = [slice(*edges[i : i + 2]) for i in range(CHUNKS)]
    firsts, lows, actives, active_lows, feed_lows, feed_others = [], [], [], [], [], []
    done = context_whole
    for cut in cuts:
        attention = dot(after(context_whole[cut], done), out_whole, NN) + out_bias
        first = jax.vjp(
            layer_norm, tokens[cut].astype(F32) + attention, first_gain, first_shift
        )
        low = first[0].astype(BF16)
        hidden = dot(low, up_weight, NN) + up_bias.reshape(-1)
        active = jax.vjp(gelu_tanh, hidden)
        active_low = active[0].astype(BF16)
        feed_low = dot(active_low, down_weight, NN).astype(BF16)
        done = feed_low
        firsts.append(first)
        lows.append(low)
        actives.append(active)
        active_lows.append(active_low)
        feed_lows.append(feed_low)
        feed_others.append(flip(feed_low, "tensor", 0))
    seconds, second_grads, feed_grads, hidden_lows, grad_lows, grad_others = (
        [], [], [], [], [], [],
    )
    for i, cut in enumerate(cuts):
        other = after(feed_others[i], done)
        feed = feed_lows[i].astype(F32) + other.astype(F32) + down_bias
        second, second_back = jax.vjp(
            layer_norm, firsts[i][0] + feed, second_gain, second_shift
        )
        grads = second_back(cotangent[cut].astype(F32))
        feed_grad = grads[0].astype(BF16)
        hidden_low = actives[i][1](dot(feed_grad, down_weight, NT))[0].astype(BF16)
        grad_low = dot(hidden_low, up_weight, NT).astype(BF16)
        done = grad_low
        seconds.append(second.astype(BF16))
        second_grads.append(grads)
        feed_grads.append(feed_grad)
        hidden_lows.append(hidden_low)
        grad_lows.append(grad_low)
        grad_others.append(flip(grad_low, "tensor", 0))
    layer_output = jnp.concatenate(seconds, axis=0)
    feed_grad = after(jnp.concatenate(feed_grads, axis=0), done)
    active_low = jnp.concatenate(active_lows, axis=0)
    down_rows = dot(feed_grad, active_low, TN).astype(BF16)
    down_scatter = Scatter(down_rows, BF16)
    down_flight = down_scatter.fly()
    hidden_low = after(jnp.concatenate(hidden_lows, axis=0), down_rows)
    first_low = jnp.concatenate(lows, axis=0)
    up_rows = dot(first_low, hidden_low, TN).astype(BF16)
    up_scatter = Scatter(up_rows, BF16, True)
    up_flight = up_scatter.fly()
    downbias_grad = column_sums(feed_grad)
    upbias_grad = column_sums(hidden_low)
    secondgain_grad = sum(grads[1] for grads in second_grads)
    secondshift_grad = sum(grads[2] for grads in second_grads)
    done = down_scatter.gather(after(down_flight, up_rows))
    middle = down_rows.shape[1] // 2
    down_parts = [
        Columns(down_scatter, slice(None, middle)),
        Columns(down_scatter, slice(middle, None), True),
    ]

    attention_backs, firstgain_parts, firstshift_parts = [], [], []
    for i in range(CHUNKS):
        other = after(grad_others[i], done)
        grad = second_grads[i][0] + (grad_lows[i].astype(F32) + other.astype(F32))
        grads = firsts[i][1](grad)
        attention_backs.append(grads[0])
        firstgain_parts.append(grads[1])
        firstshift_parts.append(grads[2])
    attention_back = jnp.concatenate(attention_backs, axis=0)
    firstgain_grad = sum(firstgain_parts)
    firstshift_grad = sum(firstshift_parts)
    attention_grad = attention_back.astype(BF16)
    outbias_grad = column_sums(attention_grad)
    context_grad = dot(attention_grad, out_weight, NT).astype(BF16)
    out_rows = dot(attention_grad, context, TN).astype(BF16)
    out_scatter = Scatter(out_rows, BF16)
    up_scatter.land(after(up_flight, out_rows))

    size = lax.axis_size("dp")

    def by_dp(vector, leading):
        return (
            vector.reshape(leading, size, -1).transpose(1, 0, 2).reshape(size, -1)
        )

    def unpack(packed, pieces):
        vectors, at = [], 0
        for part, leading in pieces:
            piece = packed[at : at + part.shape[1]]
            at += part.shape[1]
            vectors.append(piece.reshape(leading, -1) if leading else piece)
        return vectors

    units = up_bias.shape[0]
    early = [
        (by_dp(outbias_grad, 1), 0),
        (by_dp(firstgain_grad, 1), 0),
        (by_dp(firstshift_grad, 1), 0),
        (by_dp(upbias_grad, units), units),
        (by_dp(downbias_grad, 1), 0),
        (by_dp(secondgain_grad, 1), 0),
        (by_dp(secondshift_grad, 1), 0),
    ]
    early_scatter = Scatter(jnp.concatenate([part for part, _ in early], axis=1), F32)

    tokens_turned = tokens.T
    trips = [[(0, 0), (0, 1), (2, 0), (1, 1)], [(1, 0)], [(2, 1)], [(2, 2)]]
    ahead = [ahead[:, i * LANES : (i + 1) * LANES] for i in range(3)]
    other_weights = [[None] * 2, [None, None, ahead[0]], [None] * 3, ahead[1:]]
    joined, others, sums, proj_scatters = [], [], [], []
    active = [up_scatter, out_scatter, early_scatter, down_parts[0]]
    for group in range(groups):
        cargo = [scatter.cargo for scatter in active]
        cargo += [(weights[place][piece], across) for place, piece in trips[group]]
        if group > 0:
            cargo.append((joined[-1], across))
        out, lse = outs[group]
        rows_back, row_sums, keep, outgoing, *arrived = attend_back(
            queries,
            context_grad,
            tokens_turned,
            group,
            out,
            lse,
            blocks[group],
            scale,
            cargo,
            group,
        )
        for scatter in active:
            scatter.land(arrived.pop(0))
        for place, piece in trips[group]:
            other_weights[place][piece] = arrived.pop(0)
        if group > 0:
            others.append(arrived.pop(0))
        joined.append(rows_back)
        sums.append(row_sums.reshape(3, LANES))
        proj_scatters.append(Ready(keep, outgoing, group < groups - 1))
        active.append(proj_scatters[-1])
        if group == 1:
            active.append(down_parts[1])
        active = [scatter for scatter in active if scatter.cargo is not None]
    sums = jnp.stack(sums, axis=1).reshape(3, local)
    late = [(by_dp(sums[0], heads), heads), (by_dp(sums[2], heads), heads)]
    late_rows = jnp.concatenate([part for part, _ in late], axis=1)
    late_rows = jnp.pad(late_rows[:, None, :], ((0, 0), (0, 7), (0, 0)))
    late_scatter = Scatter(late_rows.reshape(8 * size, -1), F32)
    active.append(late_scatter)

    tokens_grad, proj_grad, *ends = tail(
        joined,
        others,
        weights,
        other_weights,
        attention_backs,
        active,
        proj_scatters,
        groups,
    )
    for scatter in active:
        if scatter not in proj_scatters:
            scatter.whole = ends.pop(0)
    outweight_grad = out_scatter.result()
    upweight_grad = up_scatter.result()
    downweight_grad = jnp.concatenate([part.result() for part in down_parts], axis=1)
    vectors = unpack(late_scatter.result()[0], late) + unpack(
        early_scatter.result()[0], early
    )
    return (
        layer_output,
        tokens_grad,
        proj_grad.reshape(width // size, 3, local),
        vectors[0],
        vectors[1],
        outweight_grad.T,
        vectors[2],
        vectors[3],
        vectors[4],
        upweight_grad,
        vectors[5],
        downweight_grad.T,
        vectors[6],
        vectors[7],
        vectors[8],
    )


def solution(mesh):
    return jax.shard_map(
        body,
        mesh=mesh,
        in_specs=(
            P("dp", None),
            P(None, None, "tensor"),
            P("tensor", None),
            P("tensor", None),
            P("tensor", None),
            P(),
            P(),
            P(),
            P(None, "tensor"),
            P("tensor", None),
            P("tensor", None),
            P(),
            P(),
            P(),
            P("dp", None),
        ),
        out_specs=(
            P("dp", None),
            P("dp", None),
            P("dp", None, "tensor"),
            P("tensor", "dp"),
            P("tensor", "dp"),
            P("tensor", "dp"),
            P("dp"),
            P("dp"),
            P("dp"),
            P("dp", "tensor"),
            P("tensor", "dp"),
            P("tensor", "dp"),
            P("dp"),
            P("dp"),
            P("dp"),
        ),
        check_vma=False,
    )
```

```python
import functools
import math

import jax
import jax.numpy as jnp
from jax import lax
from jax.experimental import pallas as pl
from jax.experimental.pallas import tpu as pltpu
from jax.sharding import PartitionSpec as P

EPS = 1e-12
F32 = jnp.float32
BF16 = jnp.bfloat16
LANES = 128
HALF = 64
SOURCES = 4
CHUNKS = 3
NN = (((1,), (0,)), ((), ()))
NT = (((1,), (1,)), ((), ()))
TN = (((0,), (0,)), ((), ()))
MESH = pl.DeviceIdType.MESH


def dot(left, right, dims):
    return lax.dot_general(left, right, dims, preferred_element_type=F32)


def flip(value, axis, bit):
    pairs = [(source, source ^ (1 << bit)) for source in range(lax.axis_size(axis))]
    return lax.ppermute(value, axis, pairs)


def pair_sum(partial):
    low = partial.astype(BF16)
    return low.astype(F32) + flip(low, "tensor", 0).astype(F32)


def partner(axis, bit):
    place = lax.axis_index(axis)
    return {axis: place + (1 - 2 * (place // (1 << bit) % 2)) * (1 << bit)}


def greet(links):
    barrier = pltpu.get_barrier_semaphore()
    for axis, bit in links:
        pl.semaphore_signal(
            barrier, inc=1, device_id=partner(axis, bit), device_id_type=MESH
        )
    pl.semaphore_wait(barrier, len(links))


def send(source, target, semaphores, index, axis, bit):
    return pltpu.make_async_remote_copy(
        src_ref=source,
        dst_ref=target,
        send_sem=semaphores.at[0, index],
        recv_sem=semaphores.at[1, index],
        device_id=partner(axis, bit),
        device_id_type=MESH,
    )


def after(value, *earlier):
    return lax.optimization_barrier((value, earlier))[0]


def sides(value, bit, left):
    view = value.reshape(1 << left.index(bit), 2, -1, value.shape[-1])
    own = lax.axis_index("dp") >> bit & 1
    return [
        lax.dynamic_index_in_dim(view, side, 1, keepdims=False).reshape(
            -1, view.shape[-1]
        )
        for side in (own, 1 - own)
    ]


class Scatter:
    def __init__(self, rows, wire, far_first=False):
        size = lax.axis_size("dp")
        bits = size.bit_length() - 1
        self.part = rows.shape[0] // size
        self.whole = rows
        self.wire = wire
        self.left = list(range(bits))[::-1]
        self.order = list(range(bits))
        if far_first and bits > 2:
            self.order = [0] + self.order[2:] + [1]
        self.split()

    def split(self, ready=None):
        self.cargo = None
        if not self.order:
            return
        bit = self.order.pop(0)
        if ready is None:
            ready = sides(self.whole, bit, self.left)
        self.left.remove(bit)
        self.keep = ready[0]
        self.cargo = (ready[1].astype(self.wire), ("dp", bit))

    def gather(self, arrived):
        self.whole = self.keep.astype(F32) + arrived.astype(F32)
        return self.whole

    def land(self, arrived):
        if not self.order:
            self.cargo = None
            return self.gather(arrived)
        bit = self.order[0]
        kept, sent = sides(self.keep, bit, self.left), sides(arrived, bit, self.left)
        self.split([a.astype(F32) + b.astype(F32) for a, b in zip(kept, sent)])

    def fly(self):
        value, (axis, bit) = self.cargo
        return flip(value, axis, bit)

    def result(self):
        return self.whole


class Columns(Scatter):
    def __init__(self, other, cols, far_first=False):
        self.part, self.wire = other.part, other.wire
        self.left, self.order = list(other.left), list(other.order)
        if far_first and len(self.order) > 1:
            self.order = self.order[1:] + self.order[:1]
        self.whole = other.whole[:, cols]
        self.split()


class Ready(Scatter):
    def __init__(self, keep, out, far_first):
        size = lax.axis_size("dp")
        bits = size.bit_length() - 1
        self.part = 2 * keep.shape[0] // size
        self.wire = out.dtype
        self.left = list(range(bits))[::-1]
        self.order = list(range(bits))
        if far_first and bits > 2:
            self.order = [0] + self.order[2:] + [1]
        self.split([keep, out])


def layer_norm(rows, gain, shift):
    mean = jnp.mean(rows, axis=-1, keepdims=True)
    centered = rows - mean
    spread = jnp.mean(centered * centered, axis=-1, keepdims=True)
    return centered * lax.rsqrt(spread + EPS) * gain + shift


def gelu_tanh(values):
    return jax.nn.gelu(values, approximate=True)


def column_sums(values):
    return dot(jnp.ones((16, values.shape[0]), BF16), values, NN)[0]


def head_lanes(shape, head):
    lane = lax.broadcasted_iota(jnp.int32, shape, 1)
    return (lane < HALF) if head == 0 else (lane >= HALF)


def forward_kernel(scale, tile, *refs):
    q_ref = refs[0]
    k_refs = refs[1 : 1 + SOURCES]
    v_refs = refs[1 + SOURCES : 1 + 2 * SOURCES]
    o_ref, lse_ref, s_ref, vt_ref = refs[1 + 2 * SOURCES :]
    span = k_refs[0].shape[0]

    @pl.when(pl.program_id(0) == 0)
    def _():
        for source in range(SOURCES):
            vt_ref[:LANES, source * span : (source + 1) * span] = jnp.transpose(
                v_refs[source][...]
            )
        vt_ref[LANES:, :] = jnp.ones((vt_ref.shape[0] - LANES, vt_ref.shape[1]), BF16)

    q = q_ref[...] * scale
    outs = []
    for head in range(2):
        own = head_lanes(q.shape, head)
        qt = jnp.transpose(jnp.where(own, q, jnp.zeros_like(q)))
        peak = None
        for source in range(SOURCES):
            for start in range(0, span, tile):
                scores = dot(k_refs[source][start : start + tile, :], qt, NN)
                base = source * span + start
                s_ref[head, base : base + tile, :] = scores
                top = jnp.max(scores, axis=0, keepdims=True)
                peak = top if peak is None else jnp.maximum(peak, top)
        total = None
        for start in range(0, SOURCES * span, tile):
            weights = jnp.exp(s_ref[head, start : start + tile, :] - peak).astype(BF16)
            part = dot(vt_ref[:, start : start + tile], weights, NN)
            total = part if total is None else total + part
        mass = total[LANES : LANES + 1, :]
        outs.append(total[head * HALF : (head + 1) * HALF, :] / mass)
        lse_ref[head, :] = (peak + jnp.log(mass))[0]
    o_ref[...] = jnp.transpose(jnp.concatenate(outs, 0))


def attend(queries, group, blocks, scale):
    rows = queries.shape[0]
    span = blocks[0].shape[0]
    tq = rows // 2
    keys = SOURCES * span
    return pl.pallas_call(
        functools.partial(forward_kernel, scale, span // 2),
        grid=(rows // tq,),
        in_specs=[pl.BlockSpec((tq, LANES), lambda i: (i, group))]
        + [pl.BlockSpec((span, LANES), lambda i: (0, 0))] * SOURCES
        + [pl.BlockSpec((span, LANES), lambda i: (0, 1))] * SOURCES,
        out_specs=[
            pl.BlockSpec((tq, LANES), lambda i: (i, 0)),
            pl.BlockSpec((2, tq), lambda i: (0, i)),
        ],
        out_shape=[
            jax.ShapeDtypeStruct((rows, LANES), F32),
            jax.ShapeDtypeStruct((2, rows), F32),
        ],
        scratch_shapes=[
            pltpu.VMEM((2, keys, tq), F32),
            pltpu.VMEM((LANES + 16, keys), BF16),
        ],
        compiler_params=pltpu.CompilerParams(vmem_limit_bytes=40 << 20),
        cost_estimate=pl.CostEstimate(
            flops=16 * rows * keys * LANES,
            bytes_accessed=4 * (keys + rows) * LANES + 4 * rows * LANES,
            transcendentals=2 * rows * keys,
        ),
        name="attend",
    )(queries, *blocks, *blocks)


def thirds(value):
    high = value.astype(BF16).astype(F32)
    rest = value - high
    middle = rest.astype(BF16).astype(F32)
    return high, middle, rest - middle


def backward_kernel(scale, tile, links, *refs):
    count = len(links)
    q_ref, g_ref, o_ref, lse_ref = refs[:4]
    k_refs = refs[4 : 4 + SOURCES]
    v_refs = refs[4 + SOURCES : 4 + 2 * SOURCES]
    tokens_ref = refs[4 + 2 * SOURCES]
    refs = refs[5 + 2 * SOURCES :]
    cargo_refs, refs = refs[:count], refs[count:]
    joined_ref, sums_ref, keep_ref, out_ref = refs[:4]
    landing_refs, refs = refs[4 : 4 + count], refs[4 + count :]
    qt_ref, gt_ref, dqt_ref, k_ref, v_ref, d_ref = refs[:6]
    diagonal_ref, cross_ref, beside_ref = refs[6:9]
    diagonal_in, cross_in, beside_in, product_ref, turned_ref, semaphores, local = refs[9:]
    turned_copy = pltpu.make_async_copy(tokens_ref, turned_ref, local.at[0])
    step = pl.program_id(0)
    rows = q_ref.shape[0]
    own_links = [("dp", 0), ("dp", 1)]
    copies = [
        send(cargo_refs[i], landing_refs[i], semaphores, i, *links[i])
        for i in range(count)
    ]
    halves = [slice(half * tile, (half + 1) * tile) for half in range(2)]

    def part_copies(source, target, first, bit):
        return [
            send(source.at[rows], target.at[rows], semaphores, count + first + i, "dp", bit)
            for i, rows in enumerate(halves)
        ]

    diagonal_copies = part_copies(diagonal_ref, diagonal_in, 0, 0)
    cross_copies = part_copies(cross_ref, cross_in, 2, 1)
    beside_copies = part_copies(beside_ref, beside_in, 4, 0)

    @pl.when(step == 0)
    def _():
        greet(sorted(set(own_links + links)))
        for copy in copies:
            copy.start()
        turned_copy.start()
        q = q_ref[...] * scale
        g = g_ref[...]
        products = jnp.transpose(g.astype(F32) * o_ref[...])
        row = lax.broadcasted_iota(jnp.int32, (LANES, rows), 0)
        for head in range(2):
            own = head_lanes(q.shape, head)
            qt_ref[head, :LANES, :] = jnp.transpose(jnp.where(own, q, jnp.zeros_like(q)))
            gt_ref[head, :LANES, :] = jnp.transpose(jnp.where(own, g, jnp.zeros_like(g)))
            centre = jnp.sum(
                products[head * HALF : (head + 1) * HALF], axis=0, keepdims=True
            )
            for ref, value in (
                (qt_ref, -lse_ref[head : head + 1, :]),
                (gt_ref, -centre),
            ):
                high, middle, low = thirds(value)
                ref[head, LANES:, :] = jnp.where(
                    row == 0,
                    high,
                    jnp.where(row == 1, middle, jnp.where(row == 2, low, 0.0)),
                ).astype(BF16)
        dqt_ref[...] = jnp.zeros_like(dqt_ref)

    for first, later in ((1, diagonal_copies), (3, cross_copies), (5, beside_copies)):
        for half in range(2):

            @pl.when(step == first + half)
            def _():
                later[half].start()

    for source in range(SOURCES):
        for half in range(2):

            @pl.when(step == 2 * (SOURCES - 1 - source) + half)
            def _():
                k_ref[...] = k_refs[source][halves[half], :]
                v_ref[...] = v_refs[source][halves[half], :]

    k = k_ref[...]
    v = v_ref[...]
    one = jnp.ones_like(k)
    k_wide = jnp.concatenate([k, one], 1)
    v_wide = jnp.concatenate([v, one], 1)
    kt = jnp.transpose(k)
    parts = []
    for head in range(2):
        probs = jnp.exp(dot(k_wide, qt_ref[head], NN))
        centred = dot(v_wide, gt_ref[head], NN)
        score_grad = (probs * centred).astype(BF16)
        parts.append(
            (
                dot(score_grad, q_ref[...], NN),
                dot(probs.astype(BF16), g_ref[...], NN),
            )
        )
        dqt_ref[head * HALF : (head + 1) * HALF, :] += dot(
            kt[head * HALF : (head + 1) * HALF, :], score_grad, NN
        )
    first = head_lanes(k.shape, 0)
    d_ref[:, :LANES] = (jnp.where(first, parts[0][0], parts[1][0]) * scale).astype(BF16)
    d_ref[:, LANES:] = jnp.where(first, parts[0][1], parts[1][1]).astype(BF16)

    for half in range(2):
        band = halves[half]

        @pl.when(step == half)
        def _():
            diagonal_ref[band, :] = d_ref[...]

        @pl.when(step == 2 + half)
        def _():
            diagonal_copies[half].wait()
            cross_ref[band, :] = (
                d_ref[...].astype(F32) + diagonal_in[band, :].astype(F32)
            ).astype(BF16)

        @pl.when(step == 4 + half)
        def _():
            beside_ref[band, :] = d_ref[...]

        @pl.when(step == 6 + half)
        def _():
            beside_copies[half].wait()
            cross_copies[half].wait()
            joined_ref[band, LANES:] = (
                d_ref[...].astype(F32)
                + beside_in[band, :].astype(F32)
                + cross_in[band, :].astype(F32)
            ).astype(BF16)

    @pl.when(step == 7)
    def _():
        joined_ref[:, :LANES] = (jnp.transpose(dqt_ref[...]) * scale).astype(BF16)
        joined = joined_ref[...]
        sums_ref[...] = jnp.sum(joined.astype(F32), axis=0, keepdims=True)
        turned_copy.wait()
        pairs, _, part, _ = product_ref.shape
        for pair in range(0, pairs, 2):
            band = turned_ref[2 * pair * part : 2 * (pair + 2) * part, :]
            product_ref[pair : pair + 2] = (
                dot(band, joined, NN).astype(BF16).reshape(2, 2, part, 3 * LANES)
            )
        side = lax.axis_index("dp") % 2
        keep_ref[...] = product_ref[:, side].reshape(keep_ref.shape)
        out_ref[...] = product_ref[:, 1 - side].reshape(out_ref.shape)
        for copy in copies:
            copy.wait()


def attend_back(
    queries, grads, tokens, group, context, lse, blocks, scale, cargo, collective_id
):
    rows = queries.shape[0]
    span = blocks[0].shape[0]
    keys = SOURCES * span
    size, width = lax.axis_size("dp"), tokens.shape[0]
    whole = lambda i: (0, 0)
    links = [link for _, link in cargo]
    values = [value for value, _ in cargo]
    anywhere = pl.BlockSpec(memory_space=pl.ANY)
    return pl.pallas_call(
        functools.partial(backward_kernel, scale, span // 2, links),
        grid=(2 * SOURCES,),
        in_specs=[
            pl.BlockSpec((rows, LANES), lambda i: (0, group)),
            pl.BlockSpec((rows, LANES), lambda i: (0, group)),
            pl.BlockSpec((rows, LANES), whole),
            pl.BlockSpec((2, rows), whole),
        ]
        + [pl.BlockSpec((span, LANES), whole)] * SOURCES
        + [pl.BlockSpec((span, LANES), lambda i: (0, 1))] * SOURCES
        + [anywhere] * (1 + len(values)),
        out_specs=[
            pl.BlockSpec((rows, 3 * LANES), whole),
            pl.BlockSpec((1, 3 * LANES), whole),
            pl.BlockSpec((width // 2, 3 * LANES), whole),
            pl.BlockSpec((width // 2, 3 * LANES), whole),
        ]
        + [anywhere] * len(values),
        out_shape=[
            jax.ShapeDtypeStruct((rows, 3 * LANES), BF16),
            jax.ShapeDtypeStruct((1, 3 * LANES), F32),
            jax.ShapeDtypeStruct((width // 2, 3 * LANES), BF16),
            jax.ShapeDtypeStruct((width // 2, 3 * LANES), BF16),
        ]
        + [jax.ShapeDtypeStruct(v.shape, v.dtype) for v in values],
        scratch_shapes=[
            pltpu.VMEM((2, 2 * LANES, rows), BF16),
            pltpu.VMEM((2, 2 * LANES, rows), BF16),
            pltpu.VMEM((LANES, rows), F32),
            pltpu.VMEM((span // 2, LANES), BF16),
            pltpu.VMEM((span // 2, LANES), BF16),
            pltpu.VMEM((span // 2, 2 * LANES), BF16),
        ]
        + [pltpu.VMEM((span, 2 * LANES), BF16)] * 6
        + [pltpu.VMEM((size // 2, 2, width // size, 3 * LANES), BF16)]
        + [pltpu.VMEM(tokens.shape, BF16)]
        + [pltpu.SemaphoreType.DMA((2, len(values) + 6)), pltpu.SemaphoreType.DMA((1,))],
        compiler_params=pltpu.CompilerParams(
            vmem_limit_bytes=60 << 20,
            collective_id=collective_id,
            has_side_effects=True,
        ),
        cost_estimate=pl.CostEstimate(
            flops=28 * rows * keys * LANES,
            bytes_accessed=8 * keys * LANES + 12 * rows * LANES,
            transcendentals=2 * rows * keys,
        ),
        name="attend_back",
    )(queries, grads, context, lse, *blocks, *blocks, tokens, *values)


def tail_kernel(plans, widths, merged, *refs):
    chains = len(plans)
    groups = len(widths)
    pieces = sum(len(part) for part in widths)
    last = groups - 1
    last_piece = widths[last][-1]
    wide = 3 * LANES

    def take(number):
        nonlocal refs
        taken, refs = refs[:number], refs[number:]
        return taken

    joined_refs, other_refs = take(groups), take(last)
    own_weights, other_weights, base_refs = take(pieces), take(pieces - 1), take(CHUNKS)
    keep_refs, cargo_refs = take(chains), take(chains)
    total_ref = take(1)[0]
    merged_ref = take(1)[0]
    result_refs = list(take(chains - len(merged)))
    result_refs = [
        None if chain in merged else result_refs.pop(0) for chain in range(chains)
    ]
    rows_refs, weight_refs, last_rows, last_weights = take(2), take(2), take(2), take(2)
    base_ref = take(1)[0]
    hops = [[take(3) for _ in plan] for plan in plans]
    semaphores, local = refs
    links = sorted({("dp", bit) for plan in plans for bit, _, _ in plan} | {("tensor", 0)})
    greet(links)
    last_copy = send(joined_refs[last], last_rows[1], semaphores, 0, "tensor", 0)
    last_copy.start()
    weight_copy = send(
        own_weights[pieces - 1],
        last_weights[1].at[:, wide - last_piece :],
        semaphores,
        1,
        "tensor",
        0,
    )
    weight_copy.start()
    count = 2
    flights = []
    for chain, plan in enumerate(plans):
        flights.append([])
        for level, (bit, _, _) in enumerate(plan):
            land, out, _ = hops[chain][level]
            source = cargo_refs[chain] if level == 0 else out
            flights[chain].append(send(source, land, semaphores, count, "dp", bit))
            count += 1
        flights[chain][0].start()
    loads = []

    def load(source, target):
        copy = pltpu.make_async_copy(source, target, local.at[len(loads)])
        copy.start()
        loads.append(copy)

    for group in range(last):
        cols = slice(group * wide, (group + 1) * wide)
        load(joined_refs[group], rows_refs[0].at[:, cols])
        load(other_refs[group], rows_refs[1].at[:, cols])
    for side, parts in enumerate((list(own_weights), list(other_weights))):
        for group in range(groups):
            target = last_weights[side] if group == last else weight_refs[side]
            base = 0 if group == last else group * wide
            for piece in widths[group]:
                if not parts:
                    continue
                load(parts.pop(0), target.at[:, base : base + piece])
                base += piece
    load(joined_refs[last], last_rows[0])
    top = 0
    for part in range(CHUNKS):
        height = base_refs[part].shape[0]
        load(base_refs[part], base_ref.at[top : top + height, :])
        top += height

    def advance(level):
        for chain, plan in enumerate(plans):
            if level >= len(plan):
                continue
            flights[chain][level].wait()
            land = hops[chain][level][0]
            keep = keep_refs[chain] if level == 0 else None
            if level == 0:
                held = keep[...].astype(F32)
            else:
                bit, high, low = plan[level]
                own = lax.axis_index("dp") // (1 << bit) % 2
                held = hops[chain][level][2][:, own].reshape(land.shape)
            whole = held + land[...].astype(F32)
            if level == len(plan) - 1:
                if chain not in merged:
                    result_refs[chain][...] = whole
                    continue
                for piece in range(3):
                    at = (piece * groups + merged.index(chain)) * LANES
                    merged_ref[:, at : at + LANES] = whole[
                        :, piece * LANES : (piece + 1) * LANES
                    ]
                continue
            bit, high, low = plan[level + 1]
            _, out, split = hops[chain][level + 1]
            own = lax.axis_index("dp") // (1 << bit) % 2
            split[...] = whole.reshape(split.shape)
            out[...] = split[:, 1 - own].reshape(out.shape).astype(out.dtype)
        for flight in flights:
            if level + 1 < len(flight):
                flight[level + 1].start()

    for copy in loads:
        copy.wait()
    tile = total_ref.shape[0] // 4

    def early(index, carry):
        band = pl.ds(pl.multiple_of(index * tile, tile), tile)
        total_ref[band, :] = dot(rows_refs[0][band, :], weight_refs[0][...], NT) + dot(
            rows_refs[1][band, :], weight_refs[1][...], NT
        )
        return carry

    def late(index, carry):
        band = pl.ds(pl.multiple_of(index * tile, tile), tile)
        last_part = dot(last_rows[0][band, :], last_weights[0][...], NT) + dot(
            last_rows[1][band, :], last_weights[1][...], NT
        )
        total_ref[band, :] = base_ref[band, :] + (total_ref[band, :] + last_part)
        return carry

    depth = max(len(plan) for plan in plans)
    lax.fori_loop(0, 2, early, 0)
    advance(0)
    lax.fori_loop(2, 4, early, 0)
    for level in range(1, depth - 1):
        advance(level)
    last_copy.wait()
    weight_copy.wait()
    lax.fori_loop(0, 4, late, 0)
    advance(depth - 1)


def tail(
    joined, others, own_weights, other_weights, base, chains, merged, collective_id
):
    groups = len(joined)
    rows, wide = joined[0].shape
    width = own_weights[0][0].shape[0]
    widths = [[piece.shape[1] for piece in part] for part in own_weights]
    own_weights = [piece for part in own_weights for piece in part]
    other_weights = [piece for part in other_weights for piece in part]
    size = lax.axis_size("dp")
    plans, scratch, results = [], [], []
    for chain in chains:
        left = list(chain.left)
        high_bits = sorted(left + [chain.cargo[1][1]], reverse=True)
        count, part, cols = chain.keep.shape[0], chain.part, chain.keep.shape[1]
        plan = []
        for bit in [chain.cargo[1][1]] + chain.order:
            high = 1 << high_bits.index(bit)
            high_bits.remove(bit)
            held = part << len(high_bits)
            low = held // high
            plan.append((bit, high, low))
            scratch += [
                pltpu.VMEM((held, cols), chain.wire),
                pltpu.VMEM((held, cols), chain.wire),
                pltpu.VMEM((high, 2, low, cols), F32),
            ]
        plans.append(plan)
        if chain not in merged:
            results.append(jax.ShapeDtypeStruct((part, cols), F32))
    results.insert(0, jax.ShapeDtypeStruct((merged[0].part, groups * wide), F32))
    anywhere = pl.BlockSpec(memory_space=pl.ANY)
    inside = pl.BlockSpec(memory_space=pltpu.VMEM)
    values = [*joined, *others, *own_weights, *other_weights, *base]
    loads = 2 * (groups - 1) + 2 * len(own_weights) + CHUNKS
    hops = sum(len(plan) for plan in plans)
    return pl.pallas_call(
        functools.partial(
            tail_kernel, plans, widths, [chains.index(chain) for chain in merged]
        ),
        in_specs=[anywhere] * len(values)
        + [inside] * len(chains)
        + [anywhere] * len(chains),
        out_specs=[inside] * (1 + len(results)),
        out_shape=[jax.ShapeDtypeStruct((rows, width), F32)] + results,
        scratch_shapes=[pltpu.VMEM((rows, (groups - 1) * wide), BF16)] * 2
        + [pltpu.VMEM((width, (groups - 1) * wide), BF16)] * 2
        + [pltpu.VMEM((rows, wide), BF16)] * 2
        + [pltpu.VMEM((width, wide), BF16)] * 2
        + [pltpu.VMEM((rows, width), F32)]
        + scratch
        + [pltpu.SemaphoreType.DMA((2, hops + 2)), pltpu.SemaphoreType.DMA((loads,))],
        compiler_params=pltpu.CompilerParams(
            vmem_limit_bytes=60 << 20, collective_id=collective_id, has_side_effects=True
        ),
        cost_estimate=pl.CostEstimate(
            flops=12 * groups * rows * width * LANES,
            bytes_accessed=32 << 20,
            transcendentals=0,
        ),
        name="tail",
    )(*values, *[c.keep for c in chains], *[c.cargo[0] for c in chains])


def body(
    tokens,
    proj_weight,
    query_bias,
    value_bias,
    out_weight,
    out_bias,
    first_gain,
    first_shift,
    up_weight,
    up_bias,
    down_weight,
    down_bias,
    second_gain,
    second_shift,
    cotangent,
):
    rows, width = tokens.shape
    heads, head_size = query_bias.shape
    local = heads * head_size
    groups = local // LANES
    scale = 1.0 / math.sqrt(head_size)
    query_weight = proj_weight[:, 0, :]
    key_weight = proj_weight[:, 1, :]
    value_weight = proj_weight[:, 2, :]
    value_shift = value_bias.reshape(local)

    side = lax.axis_index("tensor")

    def in_order(own, other, dim):
        return jnp.where(
            side == 0,
            jnp.concatenate([own, other], axis=dim),
            jnp.concatenate([other, own], axis=dim),
        )

    own_blocks, blocks, weights = [], [], []
    for group in range(groups):
        cols = slice(group * LANES, (group + 1) * LANES)
        weight = jnp.concatenate([key_weight[:, cols], value_weight[:, cols]], axis=1)
        pieces = [query_weight[:, cols], weight]
        if group > 0:
            pieces[1:] = [key_weight[:, cols], value_weight[:, cols]]
        weights.append(pieces)
        shift = jnp.concatenate([jnp.zeros((LANES,), F32), value_shift[cols]])
        own_blocks.append((dot(tokens, weight, NN) + shift).astype(BF16))
    for own in own_blocks:
        across = flip(own, "dp", 1)
        blocks.append((own, flip(own, "dp", 0), across, flip(across, "dp", 0)))
    queries = (dot(tokens, query_weight, NN) + query_bias.reshape(local)).astype(BF16)
    out_other = flip(out_weight, "tensor", 0)
    out_whole = in_order(out_weight, out_other, 0)

    outs, own_context, other_context = [], [], []
    across = ("tensor", 0)
    ahead = jnp.concatenate([*weights[1][1:], *weights[3][:2]], axis=1)
    ahead = flip(ahead, "tensor", 0)
    for group in range(groups):
        if group > 0:
            queries = after(queries, outs[-1][1])
        if group == groups - 2:
            queries = after(queries, out_other)
        if group == groups - 1:
            queries = after(queries, ahead)
        out, lse = attend(queries, group, blocks[group], scale)
        outs.append((out, lse))
        own_context.append(out.astype(BF16))
        other_context.append(flip(own_context[-1], "tensor", 0))
    context = jnp.concatenate(own_context, axis=1)
    context_whole = in_order(context, jnp.concatenate(other_context, axis=1), 1)

    edges = [0, rows // 4, 3 * rows // 4, rows]
    cuts = [slice(*edges[i : i + 2]) for i in range(CHUNKS)]
    firsts, lows, actives, active_lows, feed_lows, feed_others = [], [], [], [], [], []
    done = context_whole
    for cut in cuts:
        attention = dot(after(context_whole[cut], done), out_whole, NN) + out_bias
        first = jax.vjp(
            layer_norm, tokens[cut].astype(F32) + attention, first_gain, first_shift
        )
        low = first[0].astype(BF16)
        hidden = dot(low, up_weight, NN) + up_bias.reshape(-1)
        active = jax.vjp(gelu_tanh, hidden)
        active_low = active[0].astype(BF16)
        feed_low = dot(active_low, down_weight, NN).astype(BF16)
        done = feed_low
        firsts.append(first)
        lows.append(low)
        actives.append(active)
        active_lows.append(active_low)
        feed_lows.append(feed_low)
        feed_others.append(flip(feed_low, "tensor", 0))
    seconds, second_grads, feed_grads, hidden_lows, grad_lows, grad_others = (
        [], [], [], [], [], [],
    )
    for i, cut in enumerate(cuts):
        other = after(feed_others[i], done)
        feed = feed_lows[i].astype(F32) + other.astype(F32) + down_bias
        second, second_back = jax.vjp(
            layer_norm, firsts[i][0] + feed, second_gain, second_shift
        )
        grads = second_back(cotangent[cut].astype(F32))
        feed_grad = grads[0].astype(BF16)
        hidden_low = actives[i][1](dot(feed_grad, down_weight, NT))[0].astype(BF16)
        grad_low = dot(hidden_low, up_weight, NT).astype(BF16)
        done = grad_low
        seconds.append(second.astype(BF16))
        second_grads.append(grads)
        feed_grads.append(feed_grad)
        hidden_lows.append(hidden_low)
        grad_lows.append(grad_low)
        grad_others.append(flip(grad_low, "tensor", 0))
    layer_output = jnp.concatenate(seconds, axis=0)
    feed_grad = after(jnp.concatenate(feed_grads, axis=0), done)
    active_low = jnp.concatenate(active_lows, axis=0)
    down_rows = dot(feed_grad, active_low, TN).astype(BF16)
    down_scatter = Scatter(down_rows, BF16)
    down_flight = down_scatter.fly()
    hidden_low = after(jnp.concatenate(hidden_lows, axis=0), down_rows)
    first_low = jnp.concatenate(lows, axis=0)
    up_rows = dot(first_low, hidden_low, TN).astype(BF16)
    up_scatter = Scatter(up_rows, BF16, True)
    up_flight = up_scatter.fly()
    downbias_grad = column_sums(feed_grad)
    upbias_grad = column_sums(hidden_low)
    secondgain_grad = sum(grads[1] for grads in second_grads)
    secondshift_grad = sum(grads[2] for grads in second_grads)
    done = down_scatter.gather(after(down_flight, up_rows))
    middle = down_rows.shape[1] // 2
    down_parts = [
        Columns(down_scatter, slice(None, middle)),
        Columns(down_scatter, slice(middle, None), True),
    ]

    attention_backs, firstgain_parts, firstshift_parts = [], [], []
    for i in range(CHUNKS):
        other = after(grad_others[i], done)
        grad = second_grads[i][0] + (grad_lows[i].astype(F32) + other.astype(F32))
        grads = firsts[i][1](grad)
        attention_backs.append(grads[0])
        firstgain_parts.append(grads[1])
        firstshift_parts.append(grads[2])
    attention_back = jnp.concatenate(attention_backs, axis=0)
    firstgain_grad = sum(firstgain_parts)
    firstshift_grad = sum(firstshift_parts)
    attention_grad = attention_back.astype(BF16)
    outbias_grad = column_sums(attention_grad)
    context_grad = dot(attention_grad, out_weight, NT).astype(BF16)
    out_rows = dot(attention_grad, context, TN).astype(BF16)
    out_scatter = Scatter(out_rows, BF16)
    up_scatter.land(after(up_flight, out_rows))

    size = lax.axis_size("dp")

    def by_dp(vector, leading):
        return (
            vector.reshape(leading, size, -1).transpose(1, 0, 2).reshape(size, -1)
        )

    def unpack(packed, pieces):
        vectors, at = [], 0
        for part, leading in pieces:
            piece = packed[at : at + part.shape[1]]
            at += part.shape[1]
            vectors.append(piece.reshape(leading, -1) if leading else piece)
        return vectors

    units = up_bias.shape[0]
    early = [
        (by_dp(outbias_grad, 1), 0),
        (by_dp(firstgain_grad, 1), 0),
        (by_dp(firstshift_grad, 1), 0),
        (by_dp(upbias_grad, units), units),
        (by_dp(downbias_grad, 1), 0),
        (by_dp(secondgain_grad, 1), 0),
        (by_dp(secondshift_grad, 1), 0),
    ]
    early_scatter = Scatter(jnp.concatenate([part for part, _ in early], axis=1), F32)

    tokens_turned = tokens.T
    trips = [[(0, 0), (0, 1), (2, 0)], [(1, 0)], [(2, 1)], [(2, 2)]]
    ahead = [ahead[:, i * LANES : (i + 1) * LANES] for i in range(4)]
    other_weights = [[None] * 2, [None, *ahead[:2]], [None] * 3, ahead[2:]]
    joined, others, sums, proj_scatters = [], [], [], []
    active = [up_scatter, out_scatter, early_scatter, down_parts[0]]
    for group in range(groups):
        cargo = [scatter.cargo for scatter in active]
        cargo += [(weights[place][piece], across) for place, piece in trips[group]]
        if group > 0:
            cargo.append((joined[-1], across))
        out, lse = outs[group]
        rows_back, row_sums, keep, outgoing, *arrived = attend_back(
            queries,
            context_grad,
            tokens_turned,
            group,
            out,
            lse,
            blocks[group],
            scale,
            cargo,
            group,
        )
        for scatter in active:
            scatter.land(arrived.pop(0))
        for place, piece in trips[group]:
            other_weights[place][piece] = arrived.pop(0)
        if group > 0:
            others.append(arrived.pop(0))
        joined.append(rows_back)
        sums.append(row_sums.reshape(3, LANES))
        proj_scatters.append(Ready(keep, outgoing, group < groups - 1))
        active.append(proj_scatters[-1])
        if group == 1:
            active.append(down_parts[1])
        active = [scatter for scatter in active if scatter.cargo is not None]
    sums = jnp.stack(sums, axis=1).reshape(3, local)
    late = [(by_dp(sums[0], heads), heads), (by_dp(sums[2], heads), heads)]
    late_rows = jnp.concatenate([part for part, _ in late], axis=1)
    late_rows = jnp.pad(late_rows[:, None, :], ((0, 0), (0, 7), (0, 0)))
    late_scatter = Scatter(late_rows.reshape(8 * size, -1), F32)
    active.append(late_scatter)

    tokens_grad, proj_grad, *ends = tail(
        joined,
        others,
        weights,
        other_weights,
        attention_backs,
        active,
        proj_scatters,
        groups,
    )
    for scatter in active:
        if scatter not in proj_scatters:
            scatter.whole = ends.pop(0)
    outweight_grad = out_scatter.result()
    upweight_grad = up_scatter.result()
    downweight_grad = jnp.concatenate([part.result() for part in down_parts], axis=1)
    vectors = unpack(late_scatter.result()[0], late) + unpack(
        early_scatter.result()[0], early
    )
    return (
        layer_output,
        tokens_grad,
        proj_grad.reshape(width // size, 3, local),
        vectors[0],
        vectors[1],
        outweight_grad.T,
        vectors[2],
        vectors[3],
        vectors[4],
        upweight_grad,
        vectors[5],
        downweight_grad.T,
        vectors[6],
        vectors[7],
        vectors[8],
    )


def solution(mesh):
    return jax.shard_map(
        body,
        mesh=mesh,
        in_specs=(
            P("dp", None),
            P(None, None, "tensor"),
            P("tensor", None),
            P("tensor", None),
            P("tensor", None),
            P(),
            P(),
            P(),
            P(None, "tensor"),
            P("tensor", None),
            P("tensor", None),
            P(),
            P(),
            P(),
            P("dp", None),
        ),
        out_specs=(
            P("dp", None),
            P("dp", None),
            P("dp", None, "tensor"),
            P("tensor", "dp"),
            P("tensor", "dp"),
            P("tensor", "dp"),
            P("dp"),
            P("dp"),
            P("dp"),
            P("dp", "tensor"),
            P("tensor", "dp"),
            P("tensor", "dp"),
            P("dp"),
            P("dp"),
            P("dp"),
        ),
        check_vma=False,
    )
```
